32 devices in a mesh: row: 8 (over y, x, core), col: 4 (over z).
Axes of the slice: x: 2, y: 2, z: 4, core: 2. Of those that a mesh axis runs over, the one named last changes fastest.
Arguments:
- row_geometry: float32 [4, 8, 16, 4, 2, 256], P('col', 'row'), may hold values from 0 to 1, as said below
- column_geometry: float32 [4, 2, 512], replicated, may hold values from 0 to 1
- octree_slot: int32 [4, 8, 8, 2], P('col'), may hold values from 0 to 15, as said below
- pivots: int32 [256], replicated, may hold values from 0 to 65535, as said below
- lower_inv: float32 [256, 256], replicated, as said below
- upper_inv: float32 [256, 256], replicated, as said below
Outputs:
- slab_out: float32 [8, 4, 8, 256, 512], P('row', 'col')
- upper_block: float32 [256, 256], replicated
The draws below stay inside these ranges and needn't reach their ends.
Inputs may be any that keep to these rules, and one draw needn't show every extreme that they name: For each process column q and owner d, the entries octree_slot[q, :, d, :] are each local tile number 0 to 15 once. pivots[i] lies between i and 65535. `row_geometry`: the two tiles of one tile row carry equal row geometry in their slots. `lower_inv`: unit lower triangular. `upper_inv`: upper triangular with positive diagonal.
All inputs are finite; a program needn't handle non-finite values.
Results may differ from the reference program's by a relative error of at most 0.0003.
Values sent between devices are 32-bit elements; how exact they have to be, the bound alone decides.
No kernel may reach another device: no remote copies, remote signals or barrier semaphores. Data moves between devices by JAX's collectives and lax.ppermute only.
A program may use at most 64 MiB of HBM per device.

```python
import jax
import jax.numpy as jnp
from jax import lax

TILE = 256
QUAD = 2
TRD = 8
SLAB = 512
PROC_ROWS = 8
PROC_COLS = 4
SLOTS = 2
TILE_ROWS = 256
M = 65536


def slot_table(key):
    keys = jax.random.split(jax.random.fold_in(key, 11), PROC_COLS * PROC_ROWS)
    orders = jax.vmap(lambda single: jax.random.permutation(single, 2 * TRD))(keys)
    shaped = orders.reshape(PROC_COLS, PROC_ROWS, PROC_ROWS, SLOTS)
    return jnp.transpose(shaped, (0, 2, 1, 3)).astype(jnp.int32)


def draw_octree_slot(key, part):
    return slot_table(key)


def draw_row_geometry(key, part):
    owner_geometry = jax.random.uniform(jax.random.fold_in(key, 12), (PROC_COLS, PROC_ROWS, TRD, 4, QUAD, TILE), jnp.float32)
    table = slot_table(key)
    tile_row = table // 2
    col_index = jnp.arange(PROC_COLS, dtype=jnp.int32)[:, None, None, None]
    owner_index = jnp.arange(PROC_ROWS, dtype=jnp.int32)[None, None, :, None]
    picked = owner_geometry[col_index, owner_index, tile_row]
    return picked.reshape(PROC_COLS, PROC_ROWS, PROC_ROWS * SLOTS, 4, QUAD, TILE)


def draw_pivots(key, part):
    offsets = jnp.arange(TILE, dtype=jnp.int32)
    return jax.random.randint(key, (TILE,), offsets, M, dtype=jnp.int32)


def draw_lower_inv(key, part):
    noise = jax.random.normal(key, (TILE, TILE), jnp.float32) * (0.5 / TILE ** 0.5)
    return jnp.tril(noise, -1) + jnp.eye(TILE, dtype=jnp.float32)


def draw_upper_inv(key, part):
    diagonal = jax.random.uniform(jax.random.fold_in(key, 1), (TILE,), jnp.float32, 1.0, 3.0) / TILE ** 0.5
    noise = jax.random.normal(jax.random.fold_in(key, 2), (TILE, TILE), jnp.float32) * (0.5 / TILE)
    return jnp.triu(noise, 1) + jnp.diag(diagonal)


def setup_inputs(seed: int = 0) -> dict:
    key_list = jax.random.split(jax.random.key(seed), 7)
    row_geometry = draw_row_geometry(jax.random.fold_in(key_list[6], 71), 0)
    column_geometry = jnp.clip(jax.random.uniform(key_list[1], (4, QUAD, SLAB), jnp.float32, 0.0, 1.0), 0.0, 1.0)
    octree_slot = draw_octree_slot(jax.random.fold_in(key_list[6], 71), 0)
    pivots = draw_pivots(jax.random.fold_in(key_list[6], 71), 0)
    lower_inv = draw_lower_inv(jax.random.fold_in(key_list[6], 71), 0)
    upper_inv = draw_upper_inv(jax.random.fold_in(key_list[6], 71), 0)
    return dict(row_geometry=row_geometry, column_geometry=column_geometry, octree_slot=octree_slot, pivots=pivots, lower_inv=lower_inv, upper_inv=upper_inv)


KAPPA = 9.0
SOFTEN = 0.05

def kernel_entries(row_points, column_points):
    quad_count = row_points.shape[-2]
    accumulated = None
    for row_point in range(quad_count):
        for column_point in range(quad_count):
            along_x = row_points[..., 0, row_point, :, None] - column_points[..., 0, column_point, None, :]
            along_y = row_points[..., 1, row_point, :, None] - column_points[..., 1, column_point, None, :]
            along_z = row_points[..., 2, row_point, :, None] - column_points[..., 2, column_point, None, :]
            spacing = jnp.sqrt(along_x * along_x + along_y * along_y + along_z * along_z)
            summand = row_points[..., 3, row_point, :, None] * column_points[..., 3, column_point, None, :] * jnp.cos(KAPPA * spacing) / (spacing + SOFTEN)
            accumulated = summand if accumulated is None else accumulated + summand
    return accumulated

def swap_order(pivots, length):

    def advance(index_now, ordering):
        target = pivots[index_now]
        at_step = ordering[index_now]
        at_target = ordering[target]
        return ordering.at[index_now].set(at_target).at[target].set(at_step)
    return lax.fori_loop(0, pivots.shape[0], advance, jnp.arange(length, dtype=jnp.int32))

def reference(row_geometry, column_geometry, octree_slot, pivots, lower_inv, upper_inv):
    slots_all = 2 * TRD
    arranged = row_geometry.reshape(PROC_COLS, PROC_ROWS, PROC_ROWS, SLOTS, 4, QUAD, TILE)
    arranged = jnp.transpose(arranged, (0, 2, 1, 3, 4, 5, 6)).reshape(PROC_COLS, PROC_ROWS, slots_all, 4, QUAD, TILE)
    numbers = jnp.transpose(octree_slot, (0, 2, 1, 3)).reshape(PROC_COLS, PROC_ROWS, slots_all).astype(jnp.int32)
    col_index = jnp.arange(PROC_COLS, dtype=jnp.int32)[:, None, None]
    row_index = jnp.arange(PROC_ROWS, dtype=jnp.int32)[None, :, None]
    by_owner = jnp.zeros_like(arranged).at[col_index, row_index, numbers].set(arranged)
    by_tile_row = by_owner.reshape(PROC_COLS, PROC_ROWS, TRD, 2, 4, QUAD, TILE)[:, :, :, 0]
    by_tile_row = jnp.transpose(by_tile_row, (2, 0, 1, 3, 4, 5)).reshape(TILE_ROWS, 4, QUAD, TILE)
    slab = lax.map(lambda points: kernel_entries(points, column_geometry), by_tile_row).reshape(M, SLAB)
    ordering = swap_order(pivots, M)
    permuted = jnp.take(slab, ordering, axis=0)
    highest = lax.Precision.HIGHEST
    upper_block = jnp.dot(lower_inv, permuted[:TILE, TILE:], precision=highest, preferred_element_type=jnp.float32)
    lower_panel = jnp.dot(permuted[:, :TILE], upper_inv, precision=highest, preferred_element_type=jnp.float32)
    trailing = permuted[:, TILE:] - jnp.dot(lower_panel, upper_block, precision=highest, preferred_element_type=jnp.float32)
    layout = jnp.concatenate([lower_panel, trailing], axis=1).reshape(TRD, PROC_COLS, PROC_ROWS, TILE, SLAB)
    slab_out = jnp.transpose(layout, (2, 1, 0, 3, 4))
    return (slab_out, upper_block)
```

```python
import functools
import math

import jax
import jax.numpy as jnp
from jax import lax
from jax.experimental import pallas as pl
from jax.experimental.pallas import tpu as pltpu
from jax.sharding import PartitionSpec as P

KAPPA = 9.0
SOFTEN = 0.05
HIGHEST = lax.Precision.HIGHEST

FIT = (1.99999988, -4.38646535, 1.60268206, -0.22763882)
LEAD = FIT[3]
A0, A1, A2 = FIT[0] / LEAD, FIT[1] / LEAD, FIT[2] / LEAD
TRIPLE = 3.0 / (LEAD * LEAD)
TURNS = KAPPA / (2.0 * math.pi)
SOFT_TURNS = SOFTEN * TURNS
WEIGHT = 0.5 * LEAD**3 * TURNS


def split(value, divisor):
    if divisor & (divisor - 1) == 0:
        shift = divisor.bit_length() - 1
        return lax.shift_right_logical(value, shift), value & (divisor - 1)
    return lax.div(value, divisor), lax.rem(value, divisor)


def as_column(row):
    count = row.shape[1]
    return jnp.transpose(jnp.broadcast_to(row, (8, count)))[:, :1]


def exact_dot(left, right):
    return jnp.dot(left, right, precision=HIGHEST, preferred_element_type=jnp.float32)


def pivot_place(pivots, tile, row_count, col_count):
    tiles, lanes = split(pivots, tile)
    rest, owner_row = split(tiles, row_count)
    local, owner_col = split(rest, col_count)
    return owner_row, owner_col, local, lanes


def pack_kernel(sizes, geometry, table, pivots, out, flat):
    row_count, col_count, tile, comps, slots = sizes
    me_row = lax.axis_index("row")
    me_col = lax.axis_index("col")
    quad = geometry.shape[2]
    for slot in range(row_count * slots):
        for axis in range(comps // quad):
            flat[pl.ds(slot * comps + axis * quad, quad), :] = geometry[slot, axis]
    piv = pivots[...]
    owner_row, owner_col, local, lanes = pivot_place(piv, tile, row_count, col_count)
    picker = (lax.broadcasted_iota(jnp.int32, (tile, tile), 0) == lanes).astype(jnp.float32)
    picked = exact_dot(flat[...], picker)
    top = jnp.zeros((comps, tile), jnp.float32)
    chosen = jnp.zeros((comps, tile), jnp.float32)
    for owner in range(row_count):
        for s in range(slots):
            number = table[me_row, owner, s]
            rows = (owner * slots + s) * comps
            block = flat[pl.ds(rows, comps), :]
            out[owner, pl.ds(s * comps, comps), :] = block
            hit = (owner_col == me_col) & (owner_row == owner) & (2 * local == number)
            chosen = jnp.where(hit, picked[rows : rows + comps], chosen)
            if owner == 0:
                here = jnp.full((comps, tile), (number == 0) & (me_col == 0))
                top = jnp.where(here, block, top)
    for owner in range(row_count):
        out[owner, pl.ds(slots * comps, comps), :] = top
        out[owner, pl.ds((slots + 1) * comps, comps), :] = chosen


def entries(rows, columns):
    total = None
    for column in columns:
        partial = None
        for row in rows:
            along_x = row[0] - column[0]
            along_y = row[1] - column[1]
            along_z = row[2] - column[2]
            square = along_x * along_x + along_y * along_y + along_z * along_z
            spacing = 1.0 / lax.rsqrt(square)
            scale = 1.0 / (spacing + SOFT_TURNS)
            turn = spacing - jnp.round(spacing)
            v = turn * turn
            c = ((v + A2) * v + A1) * v + A0
            value = (c * (c * c - TRIPLE)) * scale * row[3]
            partial = value if partial is None else partial + value
        partial = partial * column[3]
        total = partial if total is None else total + partial
    return total


def fill(points, base, columns, chunks, target, target_base, quad, height):
    for group in range(height // 8):
        block = points[pl.ds(base + group * 8, 8), :]
        rows = [
            [
                jnp.broadcast_to(block[:, axis * quad + a : axis * quad + a + 1], (8, 128))
                for axis in range(4)
            ]
            for a in range(quad)
        ]
        for place, chunk in enumerate(chunks):
            cols = [[columns[axis * quad + b, chunk] for axis in range(4)] for b in range(quad)]
            target[pl.ds(target_base + group * 8, 8), pl.ds(place * 128, 128)] = entries(rows, cols)


def main_kernel(
    sizes, arrived, shared, table, pivots, column_geometry, lower_inv, upper_inv,
    slab, upper_block, columns, owned, points, top_points, filled, right_high, right_low,
):
    row_count, col_count, tile, comps, slots = sizes
    quad = column_geometry.shape[1]
    me_row = lax.axis_index("row")
    me_col = lax.axis_index("col")
    t = pl.program_id(0)
    tile_rows = pl.num_programs(0)
    lane_chunks = tile // 128
    height = 16

    @pl.when(t == 0)
    def _():
        scale = [TURNS] * (3 * quad) + [WEIGHT] * quad
        for axis in range(4):
            for b in range(quad):
                for chunk in range(2 * lane_chunks):
                    part = column_geometry[axis, pl.ds(b, 1), pl.ds(chunk * 128, 128)]
                    if axis < 3:
                        part = part * TURNS
                    columns[axis * quad + b, chunk] = jnp.broadcast_to(part, (8, 128))
        for source in range(row_count):
            for s in range(slots):
                number = table[source, me_row, s]

                @pl.when(number & 1 == 0)
                def _():
                    owned[lax.shift_right_logical(number, 1)] = arrived[source, pl.ds(s * comps, comps), :]

        piv = pivots[...]
        piv_col = as_column(piv)
        owner_row, owner_col, local, lanes = pivot_place(piv, tile, row_count, col_count)
        down = lax.broadcasted_iota(jnp.int32, (tile, tile), 0)
        across = lax.broadcasted_iota(jnp.int32, (tile, tile), 1)
        same = piv_col == piv
        earlier = down < across
        line = lax.broadcasted_iota(jnp.int32, (1, tile), 1)
        before = jnp.max(jnp.where(same & earlier, down, -1), axis=0, keepdims=True)
        after = jnp.max(jnp.where(same & (down > across), 1, 0), axis=0, keepdims=True)
        parent = jnp.max(jnp.where((piv_col == across) & earlier, down, -1), axis=0, keepdims=True)
        moved = jnp.max(parent)
        root = jnp.where(parent >= 0, parent, line)

        def doubled(carry):
            _, now = carry
            pick = (down == now).astype(jnp.float32)
            new = jnp.dot(
                jnp.broadcast_to(now, (8, tile)).astype(jnp.float32), pick,
                precision=HIGHEST, preferred_element_type=jnp.float32,
            )[:1].astype(jnp.int32)
            return jnp.max(jnp.where(new != now, 1, 0)), new

        _, root = lax.while_loop(lambda carry: carry[0] > 0, doubled, (jnp.where(moved >= 0, 1, 0), root))

        top = shared[pl.ds(0, comps), :]
        chosen = shared[pl.ds(comps, comps), :]
        carried = exact_dot(top, (down == root).astype(jnp.float32))
        again = exact_dot(carried, (down == before).astype(jnp.float32))
        new_top = jnp.where(before >= 0, again, chosen)
        mine = (owner_row == me_row) & (owner_col == me_col) & (after == 0) & (piv >= tile)
        lane_col = as_column(lanes)
        place = (lane_col == across).astype(jnp.float32)
        parts = []
        for k in range(owned.shape[0]):
            parts.append(jnp.where(mine & (local == k), carried, 0.0))
        for k in range(owned.shape[0]):
            parts.append(jnp.broadcast_to(jnp.where(mine & (local == k), 1.0, 0.0), (8, tile)))
        sent = exact_dot(jnp.concatenate(parts, axis=0), place)
        factor = jnp.where(
            lax.broadcasted_iota(jnp.int32, (comps, tile), 0) < 3 * quad, TURNS, WEIGHT
        )
        leading = jnp.full((comps, tile), (me_row == 0) & (me_col == 0))
        count = owned.shape[0]
        for k in range(count):
            fresh = sent[k * comps : (k + 1) * comps]
            hit = sent[(count * comps + k * 8) : (count * comps + k * 8 + comps)] > 0.5
            mixed = jnp.where(hit, fresh, owned[k])
            if k == 0:
                mixed = jnp.where(leading, new_top, mixed)
            points[k] = jnp.transpose(mixed * factor)
        top_points[...] = jnp.transpose(new_top * factor)

        def top_step(step, carry):
            base = pl.multiple_of(step * height, height)
            fill(top_points, base, columns, range(lane_chunks, 2 * lane_chunks), filled, base, quad, height)
            return carry

        lax.fori_loop(0, tile // height, top_step, 0)
        upper = exact_dot(lower_inv[...], filled[:, :tile])
        upper_block[...] = upper
        both = jnp.concatenate([upper_inv[...], -exact_dot(upper_inv[...], upper)], axis=1)
        high = both.astype(jnp.bfloat16)
        right_high[...] = high
        right_low[...] = (both - high.astype(jnp.float32)).astype(jnp.bfloat16)

    def step(index, carry):
        base = pl.multiple_of(index * height, height)
        fill(points.at[t], base, columns, range(2 * lane_chunks), filled, base, quad, height)
        return carry

    lax.fori_loop(0, tile // height, step, 0)
    left = filled[:, :tile]
    high = left.astype(jnp.bfloat16)
    low = (left - high.astype(jnp.float32)).astype(jnp.bfloat16)
    dot = functools.partial(jnp.dot, preferred_element_type=jnp.float32)
    product = dot(high, right_low[...]) + dot(low, right_high[...]) + dot(high, right_high[...])
    slab[:, :tile] = product[:, :tile]
    slab[:, tile:] = product[:, tile:] + filled[:, tile:]


def per_device(row_geometry, column_geometry, octree_slot, pivots, lower_inv, upper_inv):
    row_count = lax.axis_size("row")
    col_count = lax.axis_size("col")
    tile = pivots.shape[0]
    slots_all, axes, quad = row_geometry.shape[2:5]
    slots = slots_all // row_count
    tile_rows = slots_all // 2
    comps = axes * quad
    sizes = (row_count, col_count, tile, comps, slots)
    geometry = row_geometry[0, 0]
    table = octree_slot[0]
    pivot_row = pivots.reshape(1, tile)
    vmem = pl.BlockSpec(memory_space=pltpu.VMEM)
    smem = pl.BlockSpec(memory_space=pltpu.SMEM)
    depth = (slots + 2) * comps
    packed = pl.pallas_call(
        functools.partial(pack_kernel, sizes),
        out_shape=jax.ShapeDtypeStruct((row_count, depth, tile), jnp.float32),
        in_specs=[vmem, smem, vmem],
        out_specs=vmem,
        scratch_shapes=[pltpu.VMEM((slots_all * comps, tile), jnp.float32)],
        name="pack",
    )(geometry, table, pivot_row)
    arrived = lax.all_to_all(packed, "row", 0, 0, tiled=True)
    shared = jnp.sum(arrived[:, slots * comps :, :], axis=0)
    step = 1
    while step < col_count:
        partner = [(j, j ^ step) for j in range(col_count)]
        shared = shared + lax.ppermute(shared, "col", partner)
        step *= 2
    slab, upper_block = pl.pallas_call(
        functools.partial(main_kernel, sizes),
        grid=(tile_rows,),
        out_shape=(
            jax.ShapeDtypeStruct((tile_rows * tile, 2 * tile), jnp.float32),
            jax.ShapeDtypeStruct((tile, tile), jnp.float32),
        ),
        in_specs=[vmem, vmem, smem, vmem, vmem, vmem, vmem],
        out_specs=(
            pl.BlockSpec((tile, 2 * tile), lambda t: (t, 0)),
            pl.BlockSpec((tile, tile), lambda t: (0, 0)),
        ),
        scratch_shapes=[
            pltpu.VMEM((comps, 2 * tile // 128, 8, 128), jnp.float32),
            pltpu.VMEM((tile_rows, comps, tile), jnp.float32),
            pltpu.VMEM((tile_rows, tile, comps), jnp.float32),
            pltpu.VMEM((tile, comps), jnp.float32),
            pltpu.VMEM((tile, 2 * tile), jnp.float32),
            pltpu.VMEM((tile, 2 * tile), jnp.bfloat16),
            pltpu.VMEM((tile, 2 * tile), jnp.bfloat16),
        ],
        name="panel",
    )(arrived, shared, table, pivot_row, column_geometry, lower_inv, upper_inv)
    return (slab.reshape(1, 1, tile_rows, tile, 2 * tile), upper_block)


def solution(mesh):
    placed = (
        P("col", "row", None, None, None, None),
        P(),
        P("col", None, None, None),
        P(),
        P(),
        P(),
    )
    return jax.shard_map(
        per_device,
        mesh=mesh,
        in_specs=placed,
        out_specs=(P("row", "col", None, None, None), P()),
        check_vma=False,
    )
```

```python
import functools
import math

import jax
import jax.numpy as jnp
from jax import lax
from jax.experimental import pallas as pl
from jax.experimental.pallas import tpu as pltpu
from jax.sharding import PartitionSpec as P

KAPPA = 9.0
SOFTEN = 0.05
HIGHEST = lax.Precision.HIGHEST

FIT = (1.99999988, -4.38646535, 1.60268206, -0.22763882)
LEAD = FIT[3]
A0, A1, A2 = FIT[0] / LEAD, FIT[1] / LEAD, FIT[2] / LEAD
TRIPLE = 3.0 / (LEAD * LEAD)
TURNS = KAPPA / (2.0 * math.pi)
SOFT_TURNS = SOFTEN * TURNS
WEIGHT = 0.5 * LEAD**3 * TURNS
NEAR = (0.007 * TURNS) ** 2
HEIGHT = 64


def split(value, divisor):
    if divisor & (divisor - 1) == 0:
        shift = divisor.bit_length() - 1
        return lax.shift_right_logical(value, shift), value & (divisor - 1)
    return lax.div(value, divisor), lax.rem(value, divisor)


def as_column(row):
    count = row.shape[1]
    return jnp.transpose(jnp.broadcast_to(row, (8, count)))[:, :1]


def exact_dot(left, right):
    return jnp.dot(left, right, precision=HIGHEST, preferred_element_type=jnp.float32)


def pivot_place(pivots, tile, row_count, col_count):
    tiles, lanes = split(pivots, tile)
    rest, owner_row = split(tiles, row_count)
    local, owner_col = split(rest, col_count)
    return owner_row, owner_col, local, lanes


def pack_kernel(sizes, geometry, table, pivots, out, flat):
    row_count, col_count, tile, comps, slots = sizes
    me_row = lax.axis_index("row")
    me_col = lax.axis_index("col")
    quad = geometry.shape[2]
    for slot in range(row_count * slots):
        for axis in range(comps // quad):
            flat[pl.ds(slot * comps + axis * quad, quad), :] = geometry[slot, axis]
    piv = pivots[...]
    owner_row, owner_col, local, lanes = pivot_place(piv, tile, row_count, col_count)
    picker = (lax.broadcasted_iota(jnp.int32, (tile, tile), 0) == lanes).astype(jnp.float32)
    picked = exact_dot(flat[...], picker)
    top = jnp.zeros((comps, tile), jnp.float32)
    chosen = jnp.zeros((comps, tile), jnp.float32)
    for owner in range(row_count):
        for s in range(slots):
            number = table[me_row, owner, s]
            rows = (owner * slots + s) * comps
            block = flat[pl.ds(rows, comps), :]
            out[owner, pl.ds(s * comps, comps), :] = block
            hit = (owner_col == me_col) & (owner_row == owner) & (2 * local == number)
            chosen = jnp.where(hit, picked[rows : rows + comps], chosen)
            if owner == 0:
                here = jnp.full((comps, tile), (number == 0) & (me_col == 0))
                top = jnp.where(here, block, top)
    for owner in range(row_count):
        out[owner, pl.ds(slots * comps, comps), :] = top
        out[owner, pl.ds((slots + 1) * comps, comps), :] = chosen


def entries(rows, columns):
    total = None
    for column in columns:
        partial = None
        for row in rows:
            along_x = row[0] - column[0]
            along_y = row[1] - column[1]
            along_z = row[2] - column[2]
            square = along_x * along_x + along_y * along_y + along_z * along_z
            spacing = 1.0 / lax.rsqrt(square)
            scale = 1.0 / (spacing + SOFT_TURNS)
            turn = spacing - jnp.round(spacing)
            v = turn * turn
            c = ((v + A2) * v + A1) * v + A0
            value = (c * (c * c - TRIPLE)) * scale * row[3]
            partial = value if partial is None else partial + value
        partial = partial * column[3]
        total = partial if total is None else total + partial
    return total


def three_parts(value):
    parts = []
    for _ in range(3):
        part = value.astype(jnp.bfloat16).astype(jnp.float32)
        parts.append(part)
        value = value - part
    return parts


def centred(geometry):
    u = (geometry - 0.5) * TURNS
    squares = u * u
    norm = squares + pltpu.roll(squares, 6, 0) + pltpu.roll(squares, 4, 0)
    return three_parts(u), three_parts(norm)


def left_features(geometry):
    parts, norms = centred(geometry)
    row = lax.broadcasted_iota(jnp.int32, geometry.shape, 0)
    stacked = jnp.where(
        row < 2,
        norms[0],
        jnp.where(
            row < 4,
            pltpu.roll(norms[1], 2, 0),
            jnp.where(row < 6, pltpu.roll(norms[2], 4, 0), 0.0),
        ),
    )
    blocks = [parts[i] for i in range(3) for _ in range(3)] + [stacked, jnp.ones_like(stacked)]
    return jnp.transpose(jnp.concatenate(blocks, axis=0)).astype(jnp.bfloat16)


def right_features(geometry, a, b):
    parts, norms = centred(geometry)
    row = lax.broadcasted_iota(jnp.int32, geometry.shape, 0)
    wanted = (row < 6) & ((row & 1) == a)
    turned = [part if a == b else pltpu.roll(part, (a - b) % 8, 0) for part in parts]
    doubled = [jnp.where(wanted, -2.0 * part, 0.0) for part in turned]
    ones = jnp.where(wanted, 1.0, 0.0)
    placed = jnp.zeros_like(ones)
    for i, norm in enumerate(norms):
        placed = jnp.where(row == i, pltpu.roll(norm, (i - b) % 8, 0) if i != b else norm, placed)
    blocks = [doubled[j] for _ in range(3) for j in range(3)] + [ones, placed]
    return jnp.concatenate(blocks, axis=0).astype(jnp.bfloat16)


def quick_entries(square, weights, column_weights, quad):
    total = None
    for b in range(quad):
        partial = None
        for a in range(quad):
            spacing = 1.0 / lax.rsqrt(square(a, b))
            scale = 1.0 / (spacing + SOFT_TURNS)
            turn = spacing - jnp.round(spacing)
            v = turn * turn
            c = ((v + A2) * v + A1) * v + A0
            value = (c * (c * c - TRIPLE)) * scale * weights[a]
            partial = value if partial is None else partial + value
        partial = partial * column_weights[b]
        total = partial if total is None else total + partial
    return total


def quick_fill(squares, points, base, columns, chunks, target, target_base, quad, height):
    nearest = None
    count = columns.shape[1]
    for group in range(height // 8):
        block = points[pl.ds(base + group * 8, 8), :]
        weights = [
            jnp.broadcast_to(block[:, 3 * quad + a : 3 * quad + a + 1], (8, 128)) for a in range(quad)
        ]
        for place, chunk in enumerate(chunks):
            loaded = {}
            for a in range(quad):
                for b in range(quad):
                    lane = ((a * quad + b) * count + chunk) * 128
                    value = squares[pl.ds(group * 8, 8), pl.ds(lane, 128)]
                    loaded[a, b] = value
                    nearest = value if nearest is None else jnp.minimum(nearest, value)
            target[pl.ds(target_base + group * 8, 8), pl.ds(place * 128, 128)] = quick_entries(
                lambda a, b: loaded[a, b], weights, [columns[3 * quad + b, chunk] for b in range(quad)], quad
            )
    return jnp.where(jnp.min(nearest) < NEAR, 1, 0)


def fill(points, base, columns, chunks, target, target_base, quad, height):
    for group in range(height // 8):
        block = points[pl.ds(base + group * 8, 8), :]
        rows = [
            [
                jnp.broadcast_to(block[:, axis * quad + a : axis * quad + a + 1], (8, 128))
                for axis in range(4)
            ]
            for a in range(quad)
        ]
        for place, chunk in enumerate(chunks):
            cols = [[columns[axis * quad + b, chunk] for axis in range(4)] for b in range(quad)]
            target[pl.ds(target_base + group * 8, 8), pl.ds(place * 128, 128)] = entries(rows, cols)


def main_kernel(
    sizes, arrived, shared, table, pivots, column_geometry, lower_inv, upper_inv,
    slab, upper_block, columns, owned, points, filled, right_high, right_low,
    column_points, left, right, *squares,
):
    row_count, col_count, tile, comps, slots = sizes
    quad = column_geometry.shape[1]
    me_row = lax.axis_index("row")
    me_col = lax.axis_index("col")
    t = pl.program_id(0)
    tile_rows = pl.num_programs(0)
    lane_chunks = tile // 128
    height = HEIGHT
    steps = tile // height
    everything = range(2 * lane_chunks)

    def distances(block, buffer):
        rows = left[pl.ds(pl.multiple_of(block * height, height), height), :]
        buffer[...] = jnp.dot(rows, right[...], preferred_element_type=jnp.float32)

    def sweep(tile_index, chunks, last):
        def again(index):
            base = pl.multiple_of(index * height, height)
            for part in range(0, height, 16):
                fill(points.at[tile_index], base + part, columns, chunks, filled, base + part, quad, 16)

        def checked(index, near):
            for part in range(2):

                @pl.when(near[part] > 0)
                def _():
                    again(index + part)

        def step(pair, near):
            index = 2 * pair
            checked(index - 2, near)
            flat = tile_index * steps + index
            found = []
            for part, (ahead, here) in enumerate(((squares[1], squares[0]), (squares[0], squares[1]))):
                distances(jnp.minimum(flat + 1 + part, last), ahead)
                base = pl.multiple_of((index + part) * height, height)
                found.append(
                    quick_fill(
                        here, points.at[tile_index], base, columns, chunks, filled, base, quad, height
                    )
                )
            return tuple(found)

        checked(steps - 2, lax.fori_loop(0, steps // 2, step, (0, 0)))

    @pl.when(t == 0)
    def _():
        for axis in range(4):
            column_points[pl.ds(axis * quad, quad), :] = column_geometry[axis]
        for a in range(quad):
            for b in range(quad):
                right[:, pl.ds((a * quad + b) * 2 * tile, 2 * tile)] = right_features(
                    column_points[...], a, b
                )
        for axis in range(4):
            for b in range(quad):
                for chunk in range(2 * lane_chunks):
                    part = column_geometry[axis, pl.ds(b, 1), pl.ds(chunk * 128, 128)]
                    if axis < 3:
                        part = part * TURNS
                    columns[axis * quad + b, chunk] = jnp.broadcast_to(part, (8, 128))
        for source in range(row_count):
            for s in range(slots):
                number = table[source, me_row, s]

                @pl.when(number & 1 == 0)
                def _():
                    owned[lax.shift_right_logical(number, 1)] = arrived[source, pl.ds(s * comps, comps), :]

        piv = pivots[...]
        piv_col = as_column(piv)
        owner_row, owner_col, local, lanes = pivot_place(piv, tile, row_count, col_count)
        down = lax.broadcasted_iota(jnp.int32, (tile, tile), 0)
        across = lax.broadcasted_iota(jnp.int32, (tile, tile), 1)
        same = piv_col == piv
        earlier = down < across
        line = lax.broadcasted_iota(jnp.int32, (1, tile), 1)
        before = jnp.max(jnp.where(same & earlier, down, -1), axis=0, keepdims=True)
        after = jnp.max(jnp.where(same & (down > across), 1, 0), axis=0, keepdims=True)
        parent = jnp.max(jnp.where((piv_col == across) & earlier, down, -1), axis=0, keepdims=True)
        moved = jnp.max(parent)
        root = jnp.where(parent >= 0, parent, line)

        def doubled(carry):
            _, now = carry
            pick = (down == now).astype(jnp.float32)
            new = jnp.dot(
                jnp.broadcast_to(now, (8, tile)).astype(jnp.float32), pick,
                precision=HIGHEST, preferred_element_type=jnp.float32,
            )[:1].astype(jnp.int32)
            return jnp.max(jnp.where(new != now, 1, 0)), new

        _, root = lax.while_loop(lambda carry: carry[0] > 0, doubled, (jnp.where(moved >= 0, 1, 0), root))

        top = shared[pl.ds(0, comps), :]
        chosen = shared[pl.ds(comps, comps), :]
        carried = exact_dot(top, (down == root).astype(jnp.float32))
        again = exact_dot(carried, (down == before).astype(jnp.float32))
        new_top = jnp.where(before >= 0, again, chosen)
        mine = (owner_row == me_row) & (owner_col == me_col) & (after == 0) & (piv >= tile)
        lane_col = as_column(lanes)
        place = (lane_col == across).astype(jnp.float32)
        parts = []
        for k in range(owned.shape[0]):
            parts.append(jnp.where(mine & (local == k), carried, 0.0))
        for k in range(owned.shape[0]):
            parts.append(jnp.broadcast_to(jnp.where(mine & (local == k), 1.0, 0.0), (8, tile)))
        sent = exact_dot(jnp.concatenate(parts, axis=0), place)
        factor = jnp.where(
            lax.broadcasted_iota(jnp.int32, (comps, tile), 0) < 3 * quad, TURNS, WEIGHT
        )
        leading = jnp.full((comps, tile), (me_row == 0) & (me_col == 0))
        count = owned.shape[0]
        for k in range(count):
            fresh = sent[k * comps : (k + 1) * comps]
            hit = sent[(count * comps + k * 8) : (count * comps + k * 8 + comps)] > 0.5
            mixed = jnp.where(hit, fresh, owned[k])
            if k == 0:
                mixed = jnp.where(leading, new_top, mixed)
            points[k] = jnp.transpose(mixed * factor)
            left[pl.ds(k * tile, tile), :] = left_features(mixed)
        points[count] = jnp.transpose(new_top * factor)
        left[pl.ds(count * tile, tile), :] = left_features(new_top)
        distances(count * steps, squares[0])
        sweep(count, range(lane_chunks, 2 * lane_chunks), count * steps + steps - 1)
        distances(0, squares[0])
        upper = exact_dot(lower_inv[...], filled[:, :tile])
        upper_block[...] = upper
        both = jnp.concatenate([upper_inv[...], -exact_dot(upper_inv[...], upper)], axis=1)
        high = both.astype(jnp.bfloat16)
        right_high[...] = high
        right_low[...] = (both - high.astype(jnp.float32)).astype(jnp.bfloat16)

    sweep(t, everything, tile_rows * steps - 1)
    lead = filled[:, :tile]
    high = lead.astype(jnp.bfloat16)
    low = (lead - high.astype(jnp.float32)).astype(jnp.bfloat16)
    dot = functools.partial(jnp.dot, preferred_element_type=jnp.float32)
    product = dot(high, right_low[...]) + dot(low, right_high[...]) + dot(high, right_high[...])
    slab[:, :tile] = product[:, :tile]
    slab[:, tile:] = product[:, tile:] + filled[:, tile:]


def per_device(row_geometry, column_geometry, octree_slot, pivots, lower_inv, upper_inv):
    row_count = lax.axis_size("row")
    col_count = lax.axis_size("col")
    tile = pivots.shape[0]
    slots_all, axes, quad = row_geometry.shape[2:5]
    slots = slots_all // row_count
    tile_rows = slots_all // 2
    comps = axes * quad
    sizes = (row_count, col_count, tile, comps, slots)
    geometry = row_geometry[0, 0]
    table = octree_slot[0]
    pivot_row = pivots.reshape(1, tile)
    vmem = pl.BlockSpec(memory_space=pltpu.VMEM)
    smem = pl.BlockSpec(memory_space=pltpu.SMEM)
    depth = (slots + 2) * comps
    packed = pl.pallas_call(
        functools.partial(pack_kernel, sizes),
        out_shape=jax.ShapeDtypeStruct((row_count, depth, tile), jnp.float32),
        in_specs=[vmem, smem, vmem],
        out_specs=vmem,
        scratch_shapes=[pltpu.VMEM((slots_all * comps, tile), jnp.float32)],
        name="pack",
    )(geometry, table, pivot_row)
    arrived = lax.all_to_all(packed, "row", 0, 0, tiled=True)
    shared = jnp.sum(arrived[:, slots * comps :, :], axis=0)
    step = 1
    while step < col_count:
        partner = [(j, j ^ step) for j in range(col_count)]
        shared = shared + lax.ppermute(shared, "col", partner)
        step *= 2
    slab, upper_block = pl.pallas_call(
        functools.partial(main_kernel, sizes),
        grid=(tile_rows,),
        out_shape=(
            jax.ShapeDtypeStruct((tile_rows * tile, 2 * tile), jnp.float32),
            jax.ShapeDtypeStruct((tile, tile), jnp.float32),
        ),
        in_specs=[vmem, vmem, smem, vmem, vmem, vmem, vmem],
        out_specs=(
            pl.BlockSpec((tile, 2 * tile), lambda t: (t, 0)),
            pl.BlockSpec((tile, tile), lambda t: (0, 0)),
        ),
        scratch_shapes=[
            pltpu.VMEM((comps, 2 * tile // 128, 8, 128), jnp.float32),
            pltpu.VMEM((tile_rows, comps, tile), jnp.float32),
            pltpu.VMEM((tile_rows + 1, tile, comps), jnp.float32),
            pltpu.VMEM((tile, 2 * tile), jnp.float32),
            pltpu.VMEM((tile, 2 * tile), jnp.bfloat16),
            pltpu.VMEM((tile, 2 * tile), jnp.bfloat16),
            pltpu.VMEM((comps, 2 * tile), jnp.float32),
            pltpu.VMEM(((tile_rows + 1) * tile, 11 * comps), jnp.bfloat16),
            pltpu.VMEM((11 * comps, quad * quad * 2 * tile), jnp.bfloat16),
            pltpu.VMEM((HEIGHT, quad * quad * 2 * tile), jnp.float32),
            pltpu.VMEM((HEIGHT, quad * quad * 2 * tile), jnp.float32),
        ],
        name="panel",
    )(arrived, shared, table, pivot_row, column_geometry, lower_inv, upper_inv)
    return (slab.reshape(1, 1, tile_rows, tile, 2 * tile), upper_block)


def solution(mesh):
    placed = (
        P("col", "row", None, None, None, None),
        P(),
        P("col", None, None, None),
        P(),
        P(),
        P(),
    )
    return jax.shard_map(
        per_device,
        mesh=mesh,
        in_specs=placed,
        out_specs=(P("row", "col", None, None, None), P()),
        check_vma=False,
    )
```

```python
import functools
import math

import jax
import jax.numpy as jnp
from jax import lax
from jax.experimental import pallas as pl
from jax.experimental.pallas import tpu as pltpu
from jax.sharding import PartitionSpec as P

KAPPA = 9.0
SOFTEN = 0.05
HIGHEST = lax.Precision.HIGHEST

FIT = (1.99999988, -4.38646535, 1.60268206, -0.22763882)
LEAD = FIT[3]
A0, A1, A2 = FIT[0] / LEAD, FIT[1] / LEAD, FIT[2] / LEAD
TRIPLE = 3.0 / (LEAD * LEAD)
TURNS = KAPPA / (2.0 * math.pi)
SOFT_TURNS = SOFTEN * TURNS
WEIGHT = 0.5 * LEAD**3 * TURNS
NEAR = (0.007 * TURNS) ** 2
HEIGHT = 64


def split(value, divisor):
    if divisor & (divisor - 1) == 0:
        shift = divisor.bit_length() - 1
        return lax.shift_right_logical(value, shift), value & (divisor - 1)
    return lax.div(value, divisor), lax.rem(value, divisor)


def as_column(row):
    count = row.shape[1]
    return jnp.transpose(jnp.broadcast_to(row, (8, count)))[:, :1]


def exact_dot(left, right):
    return jnp.dot(left, right, precision=HIGHEST, preferred_element_type=jnp.float32)


def pivot_place(pivots, tile, row_count, col_count):
    tiles, lanes = split(pivots, tile)
    rest, owner_row = split(tiles, row_count)
    local, owner_col = split(rest, col_count)
    return owner_row, owner_col, local, lanes


def pack_kernel(sizes, geometry, table, pivots, out, flat):
    row_count, col_count, tile, comps, slots = sizes
    me_row = lax.axis_index("row")
    me_col = lax.axis_index("col")
    quad = geometry.shape[2]
    for slot in range(row_count * slots):
        for axis in range(comps // quad):
            flat[pl.ds(slot * comps + axis * quad, quad), :] = geometry[slot, axis]
    piv = pivots[...]
    owner_row, owner_col, local, lanes = pivot_place(piv, tile, row_count, col_count)
    picker = (lax.broadcasted_iota(jnp.int32, (tile, tile), 0) == lanes).astype(jnp.float32)
    picked = exact_dot(flat[...], picker)
    top = jnp.zeros((comps, tile), jnp.float32)
    chosen = jnp.zeros((comps, tile), jnp.float32)
    for owner in range(row_count):
        for s in range(slots):
            number = table[me_row, s, owner]
            rows = (owner * slots + s) * comps
            block = flat[pl.ds(rows, comps), :]
            out[owner, pl.ds(s * comps, comps), :] = block
            hit = (owner_col == me_col) & (owner_row == owner) & (2 * local == number)
            chosen = jnp.where(hit, picked[rows : rows + comps], chosen)
            if owner == 0:
                here = jnp.full((comps, tile), (number == 0) & (me_col == 0))
                top = jnp.where(here, block, top)
    for owner in range(row_count):
        out[owner, pl.ds(slots * comps, comps), :] = top
        out[owner, pl.ds((slots + 1) * comps, comps), :] = chosen


def entries(rows, columns):
    total = None
    for column in columns:
        partial = None
        for row in rows:
            along_x = row[0] - column[0]
            along_y = row[1] - column[1]
            along_z = row[2] - column[2]
            square = along_x * along_x + along_y * along_y + along_z * along_z
            spacing = 1.0 / lax.rsqrt(square)
            scale = 1.0 / (spacing + SOFT_TURNS)
            turn = spacing - jnp.round(spacing)
            v = turn * turn
            c = ((v + A2) * v + A1) * v + A0
            value = (c * (c * c - TRIPLE)) * scale * row[3]
            partial = value if partial is None else partial + value
        partial = partial * column[3]
        total = partial if total is None else total + partial
    return total


def three_parts(value):
    parts = []
    for _ in range(3):
        part = value.astype(jnp.bfloat16).astype(jnp.float32)
        parts.append(part)
        value = value - part
    return parts


def centred(geometry):
    u = (geometry - 0.5) * TURNS
    squares = u * u
    norm = squares + pltpu.roll(squares, 6, 0) + pltpu.roll(squares, 4, 0)
    return three_parts(u), three_parts(norm)


def left_features(geometry):
    parts, norms = centred(geometry)
    row = lax.broadcasted_iota(jnp.int32, geometry.shape, 0)
    stacked = jnp.where(
        row < 2,
        norms[0],
        jnp.where(
            row < 4,
            pltpu.roll(norms[1], 2, 0),
            jnp.where(row < 6, pltpu.roll(norms[2], 4, 0), 0.0),
        ),
    )
    blocks = [parts[i] for i in range(3) for _ in range(3)] + [stacked, jnp.ones_like(stacked), jnp.zeros_like(stacked)]
    return jnp.transpose(jnp.concatenate(blocks, axis=0)).astype(jnp.bfloat16)


def right_features(geometry, a, b):
    parts, norms = centred(geometry)
    row = lax.broadcasted_iota(jnp.int32, geometry.shape, 0)
    wanted = (row < 6) & ((row & 1) == a)
    turned = [part if a == b else pltpu.roll(part, (a - b) % 8, 0) for part in parts]
    doubled = [jnp.where(wanted, -2.0 * part, 0.0) for part in turned]
    ones = jnp.where(wanted, 1.0, 0.0)
    placed = jnp.zeros_like(ones)
    for i, norm in enumerate(norms):
        placed = jnp.where(row == i, pltpu.roll(norm, (i - b) % 8, 0) if i != b else norm, placed)
    blocks = [doubled[j] for _ in range(3) for j in range(3)] + [ones, placed, jnp.zeros_like(ones)]
    return jnp.concatenate(blocks, axis=0).astype(jnp.bfloat16)


def quick_entries(square, weights, column_weights, quad):
    total = None
    for b in range(quad):
        partial = None
        for a in range(quad):
            near = square(a, b)
            spacing = near * lax.rsqrt(near)
            scale = 1.0 / (spacing + SOFT_TURNS)
            turn = spacing - jnp.round(spacing)
            v = turn * turn
            c = ((v + A2) * v + A1) * v + A0
            value = (c * (c * c - TRIPLE)) * scale * weights[a]
            partial = value if partial is None else partial + value
        partial = partial * column_weights[b]
        total = partial if total is None else total + partial
    return total


def quick_fill(squares, points, base, columns, chunks, target, target_base, quad, height):
    nearest = None
    count = columns.shape[1]
    for group in range(height // 8):
        block = points[pl.ds(base + group * 8, 8), :]
        weights = [
            jnp.broadcast_to(block[:, 3 * quad + a : 3 * quad + a + 1], (8, 128)) for a in range(quad)
        ]
        for place, chunk in enumerate(chunks):
            loaded = {}
            for a in range(quad):
                for b in range(quad):
                    lane = ((a * quad + b) * count + chunk) * 128
                    value = squares[pl.ds(group * 8, 8), pl.ds(lane, 128)]
                    loaded[a, b] = value
                    nearest = value if nearest is None else jnp.minimum(nearest, value)
            target[pl.ds(target_base + group * 8, 8), pl.ds(place * 128, 128)] = quick_entries(
                lambda a, b: loaded[a, b], weights, [columns[3 * quad + b, chunk] for b in range(quad)], quad
            )
    return jnp.where(jnp.min(nearest) < NEAR, 1, 0)


def fill(points, base, columns, chunks, target, target_base, quad, height):
    for group in range(height // 8):
        block = points[pl.ds(base + group * 8, 8), :]
        rows = [
            [
                jnp.broadcast_to(block[:, axis * quad + a : axis * quad + a + 1], (8, 128))
                for axis in range(4)
            ]
            for a in range(quad)
        ]
        for place, chunk in enumerate(chunks):
            cols = [[columns[axis * quad + b, chunk] for axis in range(4)] for b in range(quad)]
            target[pl.ds(target_base + group * 8, 8), pl.ds(place * 128, 128)] = entries(rows, cols)


def order_kernel(pivots, column_geometry, order, columns, right, column_points):
    quad = column_geometry.shape[1]
    tile = pivots.shape[1]
    lane_chunks = tile // 128
    for axis in range(4):
        column_points[pl.ds(axis * quad, quad), :] = column_geometry[axis]
    for a in range(quad):
        for b in range(quad):
            right[:, pl.ds((a * quad + b) * 2 * tile, 2 * tile)] = right_features(
                column_points[...], a, b
            )
    for axis in range(4):
        for b in range(quad):
            for chunk in range(2 * lane_chunks):
                part = column_geometry[axis, pl.ds(b, 1), pl.ds(chunk * 128, 128)]
                if axis < 3:
                    part = part * TURNS
                columns[axis * quad + b, chunk] = jnp.broadcast_to(part, (8, 128))
    piv = pivots[...]
    piv_col = as_column(piv)
    down = lax.broadcasted_iota(jnp.int32, (tile, tile), 0)
    across = lax.broadcasted_iota(jnp.int32, (tile, tile), 1)
    same = piv_col == piv
    earlier = down < across
    line = lax.broadcasted_iota(jnp.int32, (1, tile), 1)
    before = jnp.max(jnp.where(same & earlier, down, -1), axis=0, keepdims=True)
    after = jnp.max(jnp.where(same & (down > across), 1, 0), axis=0, keepdims=True)
    parent = jnp.max(jnp.where((piv_col == across) & earlier, down, -1), axis=0, keepdims=True)
    moved = jnp.max(parent)
    root = jnp.where(parent >= 0, parent, line)

    def doubled(carry):
        _, now = carry
        pick = (down == now).astype(jnp.float32)
        new = jnp.dot(
            jnp.broadcast_to(now, (8, tile)).astype(jnp.float32), pick,
            precision=HIGHEST, preferred_element_type=jnp.float32,
        )[:1].astype(jnp.int32)
        return jnp.max(jnp.where(new != now, 1, 0)), new

    _, root = lax.while_loop(lambda carry: carry[0] > 0, doubled, (jnp.where(moved >= 0, 1, 0), root))
    order[...] = jnp.concatenate([root, before, after] + [root] * 5, axis=0)


def main_kernel(
    sizes, arrived, shared, table, pivots, order, columns, right, lower_inv, upper_inv,
    slab, upper_block, owned, points, filled, right_high, right_low, left, *squares,
):
    row_count, col_count, tile, comps, slots = sizes
    quad = 2 * comps // 8
    me_row = lax.axis_index("row")
    me_col = lax.axis_index("col")
    t = pl.program_id(0)
    tile_rows = pl.num_programs(0)
    lane_chunks = tile // 128
    height = HEIGHT
    steps = tile // height
    everything = range(2 * lane_chunks)

    def distances(block, buffer):
        rows = left[pl.ds(pl.multiple_of(block * height, height), height), :]
        buffer[...] = jnp.dot(rows, right[...], preferred_element_type=jnp.float32)

    def sweep(tile_index, chunks, last):
        def again(index):
            base = pl.multiple_of(index * height, height)
            for part in range(0, height, 16):
                fill(points.at[tile_index], base + part, columns, chunks, filled, base + part, quad, 16)

        def checked(index, near):
            for part in range(2):

                @pl.when(near[part] > 0)
                def _():
                    again(index + part)

        def step(pair, near):
            index = 2 * pair
            checked(index - 2, near)
            flat = tile_index * steps + index
            found = []
            for part, (ahead, here) in enumerate(((squares[1], squares[0]), (squares[0], squares[1]))):
                distances(jnp.minimum(flat + 1 + part, last), ahead)
                base = pl.multiple_of((index + part) * height, height)
                found.append(
                    quick_fill(
                        here, points.at[tile_index], base, columns, chunks, filled, base, quad, height
                    )
                )
            return tuple(found)

        checked(steps - 2, lax.fori_loop(0, steps // 2, step, (0, 0)))

    @pl.when(t == 0)
    def _():
        for source in range(row_count):
            for s in range(slots):
                number = table[source, s, me_row]

                @pl.when(number & 1 == 0)
                def _():
                    owned[lax.shift_right_logical(number, 1)] = arrived[source, pl.ds(s * comps, comps), :]

        piv = pivots[...]
        owner_row, owner_col, local, lanes = pivot_place(piv, tile, row_count, col_count)
        down = lax.broadcasted_iota(jnp.int32, (tile, tile), 0)
        across = lax.broadcasted_iota(jnp.int32, (tile, tile), 1)
        root = order[pl.ds(0, 1), :]
        before = order[pl.ds(1, 1), :]
        after = order[pl.ds(2, 1), :]
        top = shared[pl.ds(0, comps), :]
        chosen = shared[pl.ds(comps, comps), :]
        carried = exact_dot(top, (down == root).astype(jnp.float32))
        again = exact_dot(carried, (down == before).astype(jnp.float32))
        new_top = jnp.where(before >= 0, again, chosen)
        mine = (owner_row == me_row) & (owner_col == me_col) & (after == 0) & (piv >= tile)
        lane_col = as_column(lanes)
        place = (lane_col == across).astype(jnp.float32)
        parts = []
        for k in range(owned.shape[0]):
            parts.append(jnp.where(mine & (local == k), carried, 0.0))
        for k in range(owned.shape[0]):
            parts.append(jnp.broadcast_to(jnp.where(mine & (local == k), 1.0, 0.0), (8, tile)))
        sent = exact_dot(jnp.concatenate(parts, axis=0), place)
        factor = jnp.where(
            lax.broadcasted_iota(jnp.int32, (comps, tile), 0) < 3 * quad, TURNS, WEIGHT
        )
        leading = jnp.full((comps, tile), (me_row == 0) & (me_col == 0))
        count = owned.shape[0]
        for k in range(count):
            fresh = sent[k * comps : (k + 1) * comps]
            hit = sent[(count * comps + k * 8) : (count * comps + k * 8 + comps)] > 0.5
            mixed = jnp.where(hit, fresh, owned[k])
            if k == 0:
                mixed = jnp.where(leading, new_top, mixed)
            points[k] = jnp.transpose(mixed * factor)
            left[pl.ds(k * tile, tile), :] = left_features(mixed)
        points[count] = jnp.transpose(new_top * factor)
        left[pl.ds(count * tile, tile), :] = left_features(new_top)
        distances(count * steps, squares[0])
        sweep(count, range(lane_chunks, 2 * lane_chunks), count * steps + steps - 1)
        distances(0, squares[0])
        upper = exact_dot(lower_inv[...], filled[:, :tile])
        upper_block[...] = upper
        both = jnp.concatenate([upper_inv[...], -exact_dot(upper_inv[...], upper)], axis=1)
        high = both.astype(jnp.bfloat16)
        right_high[...] = high
        right_low[...] = (both - high.astype(jnp.float32)).astype(jnp.bfloat16)

    sweep(t, everything, tile_rows * steps - 1)
    lead = filled[:, :tile]
    high = lead.astype(jnp.bfloat16)
    low = (lead - high.astype(jnp.float32)).astype(jnp.bfloat16)
    dot = functools.partial(jnp.dot, preferred_element_type=jnp.float32)
    product = dot(high, right_low[...]) + dot(low, right_high[...]) + dot(high, right_high[...])
    slab[:, :tile] = product[:, :tile]
    slab[:, tile:] = product[:, tile:] + filled[:, tile:]


def per_device(row_geometry, column_geometry, octree_slot, pivots, lower_inv, upper_inv):
    row_count = lax.axis_size("row")
    col_count = lax.axis_size("col")
    tile = pivots.shape[0]
    slots_all, axes, quad = row_geometry.shape[2:5]
    slots = slots_all // row_count
    tile_rows = slots_all // 2
    comps = axes * quad
    sizes = (row_count, col_count, tile, comps, slots)
    geometry = row_geometry[0, 0]
    table = jnp.swapaxes(octree_slot[0], 1, 2)
    pivot_row = pivots.reshape(1, tile)
    vmem = pl.BlockSpec(memory_space=pltpu.VMEM)
    smem = pl.BlockSpec(memory_space=pltpu.SMEM)
    depth = (slots + 2) * comps
    packed = pl.pallas_call(
        functools.partial(pack_kernel, sizes),
        out_shape=jax.ShapeDtypeStruct((row_count, depth, tile), jnp.float32),
        in_specs=[vmem, smem, vmem],
        out_specs=vmem,
        scratch_shapes=[pltpu.VMEM((slots_all * comps, tile), jnp.float32)],
        name="pack",
    )(geometry, table, pivot_row)
    arrived = lax.all_to_all(packed, "row", 0, 0, tiled=True)
    shared = jnp.sum(arrived[:, slots * comps :, :], axis=0)
    step = 1
    while step < col_count:
        partner = [(j, j ^ step) for j in range(col_count)]
        shared = shared + lax.ppermute(shared, "col", partner)
        step *= 2
    order, columns, right = pl.pallas_call(
        order_kernel,
        out_shape=(
            jax.ShapeDtypeStruct((8, tile), jnp.int32),
            jax.ShapeDtypeStruct((comps, 2 * tile // 128, 8, 128), jnp.float32),
            jax.ShapeDtypeStruct((12 * comps, quad * quad * 2 * tile), jnp.bfloat16),
        ),
        in_specs=[vmem, vmem],
        out_specs=(vmem, vmem, vmem),
        scratch_shapes=[pltpu.VMEM((comps, 2 * tile), jnp.float32)],
        name="order",
    )(pivot_row, column_geometry)
    slab, upper_block = pl.pallas_call(
        functools.partial(main_kernel, sizes),
        grid=(tile_rows,),
        out_shape=(
            jax.ShapeDtypeStruct((tile_rows * tile, 2 * tile), jnp.float32),
            jax.ShapeDtypeStruct((tile, tile), jnp.float32),
        ),
        in_specs=[vmem, vmem, smem, vmem, vmem, vmem, vmem, vmem, vmem],
        out_specs=(
            pl.BlockSpec((tile, 2 * tile), lambda t: (t, 0)),
            pl.BlockSpec((tile, tile), lambda t: (0, 0)),
        ),
        scratch_shapes=[
            pltpu.VMEM((tile_rows, comps, tile), jnp.float32),
            pltpu.VMEM((tile_rows + 1, tile, comps), jnp.float32),
            pltpu.VMEM((tile, 2 * tile), jnp.float32),
            pltpu.VMEM((tile, 2 * tile), jnp.bfloat16),
            pltpu.VMEM((tile, 2 * tile), jnp.bfloat16),
            pltpu.VMEM(((tile_rows + 1) * tile, 12 * comps), jnp.bfloat16),
            pltpu.VMEM((HEIGHT, quad * quad * 2 * tile), jnp.float32),
            pltpu.VMEM((HEIGHT, quad * quad * 2 * tile), jnp.float32),
        ],
        name="panel",
    )(arrived, shared, table, pivot_row, order, columns, right, lower_inv, upper_inv)
    return (slab.reshape(1, 1, tile_rows, tile, 2 * tile), upper_block)


def solution(mesh):
    placed = (
        P("col", "row", None, None, None, None),
        P(),
        P("col", None, None, None),
        P(),
        P(),
        P(),
    )
    return jax.shard_map(
        per_device,
        mesh=mesh,
        in_specs=placed,
        out_specs=(P("row", "col", None, None, None), P()),
        check_vma=False,
    )
```

```python
import functools
import math

import jax
import jax.numpy as jnp
from jax import lax
from jax.experimental import pallas as pl
from jax.experimental.pallas import tpu as pltpu
from jax.sharding import PartitionSpec as P

KAPPA = 9.0
SOFTEN = 0.05
HIGHEST = lax.Precision.HIGHEST

FIT = (1.99999988, -4.38646535, 1.60268206, -0.22763882)
LEAD = FIT[3]
A0, A1, A2 = FIT[0] / LEAD, FIT[1] / LEAD, FIT[2] / LEAD
TRIPLE = 3.0 / (LEAD * LEAD)
TURNS = KAPPA / (2.0 * math.pi)
SOFT_TURNS = SOFTEN * TURNS
WEIGHT = 0.5 * LEAD**3 * TURNS
NEAR = (0.003 * TURNS) ** 2
PART = 16
HEIGHT = 64


def split(value, divisor):
    if divisor & (divisor - 1) == 0:
        shift = divisor.bit_length() - 1
        return lax.shift_right_logical(value, shift), value & (divisor - 1)
    return lax.div(value, divisor), lax.rem(value, divisor)


def as_column(row):
    count = row.shape[1]
    return jnp.transpose(jnp.broadcast_to(row, (8, count)))[:, :1]


def exact_dot(left, right):
    return jnp.dot(left, right, precision=HIGHEST, preferred_element_type=jnp.float32)


def pivot_place(pivots, tile, row_count, col_count):
    tiles, lanes = split(pivots, tile)
    rest, owner_row = split(tiles, row_count)
    local, owner_col = split(rest, col_count)
    return owner_row, owner_col, local, lanes


def pack_kernel(sizes, geometry, table, pivots, out, flat):
    row_count, col_count, tile, comps, slots = sizes
    me_row = lax.axis_index("row")
    me_col = lax.axis_index("col")
    quad = geometry.shape[2]
    for slot in range(row_count * slots):
        for axis in range(comps // quad):
            flat[pl.ds(slot * comps + axis * quad, quad), :] = geometry[slot, axis]
    piv = pivots[...]
    owner_row, owner_col, local, lanes = pivot_place(piv, tile, row_count, col_count)
    picker = (lax.broadcasted_iota(jnp.int32, (tile, tile), 0) == lanes).astype(jnp.float32)
    picked = exact_dot(flat[...], picker)
    top = jnp.zeros((comps, tile), jnp.float32)
    chosen = jnp.zeros((comps, tile), jnp.float32)
    for owner in range(row_count):
        for s in range(slots):
            number = table[me_row, s, owner]
            rows = (owner * slots + s) * comps
            block = flat[pl.ds(rows, comps), :]
            out[owner, pl.ds(s * comps, comps), :] = block
            hit = (owner_col == me_col) & (owner_row == owner) & (2 * local == number)
            chosen = jnp.where(hit, picked[rows : rows + comps], chosen)
            if owner == 0:
                here = jnp.full((comps, tile), (number == 0) & (me_col == 0))
                top = jnp.where(here, block, top)
    for owner in range(row_count):
        out[owner, pl.ds(slots * comps, comps), :] = top
        out[owner, pl.ds((slots + 1) * comps, comps), :] = chosen


def entries(rows, columns):
    total = None
    for column in columns:
        partial = None
        for row in rows:
            along_x = row[0] - column[0]
            along_y = row[1] - column[1]
            along_z = row[2] - column[2]
            square = along_x * along_x + along_y * along_y + along_z * along_z
            spacing = 1.0 / lax.rsqrt(square)
            scale = 1.0 / (spacing + SOFT_TURNS)
            turn = spacing - jnp.round(spacing)
            v = turn * turn
            c = ((v + A2) * v + A1) * v + A0
            value = (c * (c * c - TRIPLE)) * scale * row[3]
            partial = value if partial is None else partial + value
        partial = partial * column[3]
        total = partial if total is None else total + partial
    return total


def three_parts(value):
    parts = []
    for _ in range(3):
        part = value.astype(jnp.bfloat16).astype(jnp.float32)
        parts.append(part)
        value = value - part
    return parts


def centred(geometry):
    u = (geometry - 0.5) * TURNS
    squares = u * u
    norm = squares + pltpu.roll(squares, 6, 0) + pltpu.roll(squares, 4, 0)
    return three_parts(u), three_parts(norm)


def left_features(geometry):
    parts, norms = centred(geometry)
    row = lax.broadcasted_iota(jnp.int32, geometry.shape, 0)
    stacked = jnp.where(
        row < 2,
        norms[0],
        jnp.where(
            row < 4,
            pltpu.roll(norms[1], 2, 0),
            jnp.where(row < 6, pltpu.roll(norms[2], 4, 0), 0.0),
        ),
    )
    blocks = [parts[i] for i in range(3) for _ in range(3)] + [stacked, jnp.ones_like(stacked), jnp.zeros_like(stacked)]
    return jnp.transpose(jnp.concatenate(blocks, axis=0)).astype(jnp.bfloat16)


def right_features(geometry, a, b):
    parts, norms = centred(geometry)
    row = lax.broadcasted_iota(jnp.int32, geometry.shape, 0)
    wanted = (row < 6) & ((row & 1) == a)
    turned = [part if a == b else pltpu.roll(part, (a - b) % 8, 0) for part in parts]
    doubled = [jnp.where(wanted, -2.0 * part, 0.0) for part in turned]
    ones = jnp.where(wanted, 1.0, 0.0)
    placed = jnp.zeros_like(ones)
    for i, norm in enumerate(norms):
        placed = jnp.where(row == i, pltpu.roll(norm, (i - b) % 8, 0) if i != b else norm, placed)
    blocks = [doubled[j] for _ in range(3) for j in range(3)] + [ones, placed, jnp.zeros_like(ones)]
    return jnp.concatenate(blocks, axis=0).astype(jnp.bfloat16)


def quick_entries(square, weights, column_weights, quad):
    total = None
    for b in range(quad):
        partial = None
        for a in range(quad):
            near = square(a, b)
            spacing = near * lax.rsqrt(near)
            scale = 1.0 / (spacing + SOFT_TURNS)
            turn = spacing - jnp.round(spacing)
            v = turn * turn
            c = ((v + A2) * v + A1) * v + A0
            value = (c * (c * c - TRIPLE)) * scale * weights[a]
            partial = value if partial is None else partial + value
        partial = partial * column_weights[b]
        total = partial if total is None else total + partial
    return total


def quick_fill(squares, points, base, columns, chunks, target, target_base, quad, height):
    found = []
    count = columns.shape[1]
    for group in range(height // 8):
        if group * 8 % PART == 0:
            nearest = None
        block = points[pl.ds(base + group * 8, 8), :]
        weights = [
            jnp.broadcast_to(block[:, 3 * quad + a : 3 * quad + a + 1], (8, 128)) for a in range(quad)
        ]
        for place, chunk in enumerate(chunks):
            loaded = {}
            for a in range(quad):
                for b in range(quad):
                    lane = ((a * quad + b) * count + chunk) * 128
                    value = squares[pl.ds(group * 8, 8), pl.ds(lane, 128)]
                    loaded[a, b] = value
                    nearest = value if nearest is None else jnp.minimum(nearest, value)
            target[pl.ds(target_base + group * 8, 8), pl.ds(place * 128, 128)] = quick_entries(
                lambda a, b: loaded[a, b], weights, [columns[3 * quad + b, chunk] for b in range(quad)], quad
            )
        if (group + 1) * 8 % PART == 0:
            found.append(jnp.where(jnp.min(nearest) < NEAR, 1, 0))
    return found


def fill(points, base, columns, chunks, target, target_base, quad, height):
    for group in range(height // 8):
        block = points[pl.ds(base + group * 8, 8), :]
        rows = [
            [
                jnp.broadcast_to(block[:, axis * quad + a : axis * quad + a + 1], (8, 128))
                for axis in range(4)
            ]
            for a in range(quad)
        ]
        for place, chunk in enumerate(chunks):
            cols = [[columns[axis * quad + b, chunk] for axis in range(4)] for b in range(quad)]
            target[pl.ds(target_base + group * 8, 8), pl.ds(place * 128, 128)] = entries(rows, cols)


def order_kernel(pivots, column_geometry, order, columns, right, column_points):
    quad = column_geometry.shape[1]
    tile = pivots.shape[1]
    lane_chunks = tile // 128
    for axis in range(4):
        column_points[pl.ds(axis * quad, quad), :] = column_geometry[axis]
    for a in range(quad):
        for b in range(quad):
            right[:, pl.ds((a * quad + b) * 2 * tile, 2 * tile)] = right_features(
                column_points[...], a, b
            )
    for axis in range(4):
        for b in range(quad):
            for chunk in range(2 * lane_chunks):
                part = column_geometry[axis, pl.ds(b, 1), pl.ds(chunk * 128, 128)]
                if axis < 3:
                    part = part * TURNS
                columns[axis * quad + b, chunk] = jnp.broadcast_to(part, (8, 128))
    piv = pivots[...]
    piv_col = as_column(piv)
    down = lax.broadcasted_iota(jnp.int32, (tile, tile), 0)
    across = lax.broadcasted_iota(jnp.int32, (tile, tile), 1)
    same = piv_col == piv
    earlier = down < across
    line = lax.broadcasted_iota(jnp.int32, (1, tile), 1)
    before = jnp.max(jnp.where(same & earlier, down, -1), axis=0, keepdims=True)
    after = jnp.max(jnp.where(same & (down > across), 1, 0), axis=0, keepdims=True)
    parent = jnp.max(jnp.where((piv_col == across) & earlier, down, -1), axis=0, keepdims=True)
    moved = jnp.max(parent)
    root = jnp.where(parent >= 0, parent, line)

    def doubled(carry):
        _, now = carry
        pick = (down == now).astype(jnp.float32)
        new = jnp.dot(
            jnp.broadcast_to(now, (8, tile)).astype(jnp.float32), pick,
            precision=HIGHEST, preferred_element_type=jnp.float32,
        )[:1].astype(jnp.int32)
        return jnp.max(jnp.where(new != now, 1, 0)), new

    _, root = lax.while_loop(lambda carry: carry[0] > 0, doubled, (jnp.where(moved >= 0, 1, 0), root))
    order[...] = jnp.concatenate([root, before, after] + [root] * 5, axis=0)


def main_kernel(
    sizes, arrived, shared, table, pivots, order, columns, right, lower_inv, upper_inv,
    slab, upper_block, owned, points, filled, right_high, right_low, left, *squares,
):
    row_count, col_count, tile, comps, slots = sizes
    quad = 2 * comps // 8
    me_row = lax.axis_index("row")
    me_col = lax.axis_index("col")
    t = pl.program_id(0)
    tile_rows = pl.num_programs(0)
    lane_chunks = tile // 128
    height = HEIGHT
    steps = tile // height
    everything = range(2 * lane_chunks)

    def distances(block, buffer):
        rows = left[pl.ds(pl.multiple_of(block * height, height), height), :]
        buffer[...] = jnp.dot(rows, right[...], preferred_element_type=jnp.float32)

    def sweep(tile_index, chunks, last):
        def again(index, part):
            base = pl.multiple_of(index * height + part * PART, PART)
            fill(points.at[tile_index], base, columns, chunks, filled, base, quad, PART)

        def checked(index, near):
            total = functools.reduce(jnp.add, near)

            @pl.when(total > 0)
            def _():
                for place, flag in enumerate(near):

                    @pl.when(flag > 0)
                    def _():
                        again(index + place // (height // PART), place % (height // PART))

        def step(pair, near):
            index = 2 * pair
            checked(index - 2, near)
            flat = tile_index * steps + index
            found = []
            for part, (ahead, here) in enumerate(((squares[1], squares[0]), (squares[0], squares[1]))):
                distances(jnp.minimum(flat + 1 + part, last), ahead)
                base = pl.multiple_of((index + part) * height, height)
                found.extend(
                    quick_fill(
                        here, points.at[tile_index], base, columns, chunks, filled, base, quad, height
                    )
                )
            return tuple(found)

        checked(steps - 2, lax.fori_loop(0, steps // 2, step, (0,) * (2 * height // PART)))

    @pl.when(t == 0)
    def _():
        for source in range(row_count):
            for s in range(slots):
                number = table[source, s, me_row]

                @pl.when(number & 1 == 0)
                def _():
                    owned[lax.shift_right_logical(number, 1)] = arrived[source, pl.ds(s * comps, comps), :]

        piv = pivots[...]
        owner_row, owner_col, local, lanes = pivot_place(piv, tile, row_count, col_count)
        down = lax.broadcasted_iota(jnp.int32, (tile, tile), 0)
        across = lax.broadcasted_iota(jnp.int32, (tile, tile), 1)
        root = order[pl.ds(0, 1), :]
        before = order[pl.ds(1, 1), :]
        after = order[pl.ds(2, 1), :]
        top = shared[pl.ds(0, comps), :]
        chosen = shared[pl.ds(comps, comps), :]
        carried = exact_dot(top, (down == root).astype(jnp.float32))
        again = exact_dot(carried, (down == before).astype(jnp.float32))
        new_top = jnp.where(before >= 0, again, chosen)
        mine = (owner_row == me_row) & (owner_col == me_col) & (after == 0) & (piv >= tile)
        lane_col = as_column(lanes)
        place = (lane_col == across).astype(jnp.float32)
        parts = []
        for k in range(owned.shape[0]):
            parts.append(jnp.where(mine & (local == k), carried, 0.0))
        for k in range(owned.shape[0]):
            parts.append(jnp.broadcast_to(jnp.where(mine & (local == k), 1.0, 0.0), (8, tile)))
        sent = exact_dot(jnp.concatenate(parts, axis=0), place)
        factor = jnp.where(
            lax.broadcasted_iota(jnp.int32, (comps, tile), 0) < 3 * quad, TURNS, WEIGHT
        )
        leading = jnp.full((comps, tile), (me_row == 0) & (me_col == 0))
        count = owned.shape[0]
        for k in range(count):
            fresh = sent[k * comps : (k + 1) * comps]
            hit = sent[(count * comps + k * 8) : (count * comps + k * 8 + comps)] > 0.5
            mixed = jnp.where(hit, fresh, owned[k])
            if k == 0:
                mixed = jnp.where(leading, new_top, mixed)
            points[k] = jnp.transpose(mixed * factor)
            left[pl.ds(k * tile, tile), :] = left_features(mixed)
        points[count] = jnp.transpose(new_top * factor)
        left[pl.ds(count * tile, tile), :] = left_features(new_top)
        distances(count * steps, squares[0])
        sweep(count, range(lane_chunks, 2 * lane_chunks), count * steps + steps - 1)
        distances(0, squares[0])
        upper = exact_dot(lower_inv[...], filled[:, :tile])
        upper_block[...] = upper
        both = jnp.concatenate([upper_inv[...], -exact_dot(upper_inv[...], upper)], axis=1)
        high = both.astype(jnp.bfloat16)
        right_high[...] = high
        right_low[...] = (both - high.astype(jnp.float32)).astype(jnp.bfloat16)

    sweep(t, everything, tile_rows * steps - 1)
    lead = filled[:, :tile]
    high = lead.astype(jnp.bfloat16)
    low = (lead - high.astype(jnp.float32)).astype(jnp.bfloat16)
    dot = functools.partial(jnp.dot, preferred_element_type=jnp.float32)
    product = dot(high, right_low[...]) + dot(low, right_high[...]) + dot(high, right_high[...])
    slab[:, :tile] = product[:, :tile]
    slab[:, tile:] = product[:, tile:] + filled[:, tile:]


def per_device(row_geometry, column_geometry, octree_slot, pivots, lower_inv, upper_inv):
    row_count = lax.axis_size("row")
    col_count = lax.axis_size("col")
    tile = pivots.shape[0]
    slots_all, axes, quad = row_geometry.shape[2:5]
    slots = slots_all // row_count
    tile_rows = slots_all // 2
    comps = axes * quad
    sizes = (row_count, col_count, tile, comps, slots)
    geometry = row_geometry[0, 0]
    table = jnp.swapaxes(octree_slot[0], 1, 2)
    pivot_row = pivots.reshape(1, tile)
    vmem = pl.BlockSpec(memory_space=pltpu.VMEM)
    smem = pl.BlockSpec(memory_space=pltpu.SMEM)
    depth = (slots + 2) * comps
    packed = pl.pallas_call(
        functools.partial(pack_kernel, sizes),
        out_shape=jax.ShapeDtypeStruct((row_count, depth, tile), jnp.float32),
        in_specs=[vmem, smem, vmem],
        out_specs=vmem,
        scratch_shapes=[pltpu.VMEM((slots_all * comps, tile), jnp.float32)],
        name="pack",
    )(geometry, table, pivot_row)
    arrived = lax.all_to_all(packed, "row", 0, 0, tiled=True)
    shared = jnp.sum(arrived[:, slots * comps :, :], axis=0)
    step = 1
    while step < col_count:
        partner = [(j, j ^ step) for j in range(col_count)]
        shared = shared + lax.ppermute(shared, "col", partner)
        step *= 2
    order, columns, right = pl.pallas_call(
        order_kernel,
        out_shape=(
            jax.ShapeDtypeStruct((8, tile), jnp.int32),
            jax.ShapeDtypeStruct((comps, 2 * tile // 128, 8, 128), jnp.float32),
            jax.ShapeDtypeStruct((12 * comps, quad * quad * 2 * tile), jnp.bfloat16),
        ),
        in_specs=[vmem, vmem],
        out_specs=(vmem, vmem, vmem),
        scratch_shapes=[pltpu.VMEM((comps, 2 * tile), jnp.float32)],
        name="order",
    )(pivot_row, column_geometry)
    slab, upper_block = pl.pallas_call(
        functools.partial(main_kernel, sizes),
        grid=(tile_rows,),
        out_shape=(
            jax.ShapeDtypeStruct((tile_rows * tile, 2 * tile), jnp.float32),
            jax.ShapeDtypeStruct((tile, tile), jnp.float32),
        ),
        in_specs=[vmem, vmem, smem, vmem, vmem, vmem, vmem, vmem, vmem],
        out_specs=(
            pl.BlockSpec((tile, 2 * tile), lambda t: (t, 0)),
            pl.BlockSpec((tile, tile), lambda t: (0, 0)),
        ),
        scratch_shapes=[
            pltpu.VMEM((tile_rows, comps, tile), jnp.float32),
            pltpu.VMEM((tile_rows + 1, tile, comps), jnp.float32),
            pltpu.VMEM((tile, 2 * tile), jnp.float32),
            pltpu.VMEM((tile, 2 * tile), jnp.bfloat16),
            pltpu.VMEM((tile, 2 * tile), jnp.bfloat16),
            pltpu.VMEM(((tile_rows + 1) * tile, 12 * comps), jnp.bfloat16),
            pltpu.VMEM((HEIGHT, quad * quad * 2 * tile), jnp.float32),
            pltpu.VMEM((HEIGHT, quad * quad * 2 * tile), jnp.float32),
        ],
        name="panel",
    )(arrived, shared, table, pivot_row, order, columns, right, lower_inv, upper_inv)
    return (slab.reshape(1, 1, tile_rows, tile, 2 * tile), upper_block)


def solution(mesh):
    placed = (
        P("col", "row", None, None, None, None),
        P(),
        P("col", None, None, None),
        P(),
        P(),
        P(),
    )
    return jax.shard_map(
        per_device,
        mesh=mesh,
        in_specs=placed,
        out_specs=(P("row", "col", None, None, None), P()),
        check_vma=False,
    )
```

```python
import functools
import math

import jax
import jax.numpy as jnp
from jax import lax
from jax.experimental import pallas as pl
from jax.experimental.pallas import tpu as pltpu
from jax.sharding import PartitionSpec as P

KAPPA = 9.0
SOFTEN = 0.05

FIT = (1.99999988, -4.38646535, 1.60268206, -0.22763882)
LEAD = FIT[3]
A0, A1, A2 = FIT[0] / LEAD, FIT[1] / LEAD, FIT[2] / LEAD
TRIPLE = 3.0 / (LEAD * LEAD)
TURNS = KAPPA / (2.0 * math.pi)
SOFT_TURNS = SOFTEN * TURNS
WEIGHT = 0.5 * LEAD**3 * TURNS
NEAR = (0.003 * TURNS) ** 2
PART = 16
HEIGHT = 64


def split(value, divisor):
    if divisor & (divisor - 1) == 0:
        shift = divisor.bit_length() - 1
        return lax.shift_right_logical(value, shift), value & (divisor - 1)
    return lax.div(value, divisor), lax.rem(value, divisor)


def as_column(row):
    count = row.shape[1]
    return jnp.transpose(jnp.broadcast_to(row, (8, count)))[:, :1]


def three_parts(value):
    parts = []
    for _ in range(3):
        part = value.astype(jnp.bfloat16).astype(jnp.float32)
        parts.append(part)
        value = value - part
    return parts


def select_dot(values, choice):
    count = values.shape[0]
    stacked = jnp.concatenate(three_parts(values), axis=0).astype(jnp.bfloat16)
    product = jnp.dot(stacked, choice, preferred_element_type=jnp.float32)
    return product[:count] + product[count : 2 * count] + product[2 * count :]


def split_dot(left, right):
    dot = functools.partial(jnp.dot, preferred_element_type=jnp.float32)
    left_high, left_low = two_parts(left)
    right_high, right_low = two_parts(right)
    return dot(left_high, right_low) + dot(left_low, right_high) + dot(left_high, right_high)


def two_parts(value):
    high = value.astype(jnp.bfloat16)
    return high, (value - high.astype(jnp.float32)).astype(jnp.bfloat16)


def chosen_where(mask):
    return jnp.where(mask, 1.0, 0.0).astype(jnp.bfloat16)


def pivot_place(pivots, tile, row_count, col_count):
    tiles, lanes = split(pivots, tile)
    rest, owner_row = split(tiles, row_count)
    local, owner_col = split(rest, col_count)
    return owner_row, owner_col, local, lanes


def pack_kernel(sizes, geometry, table, pivots, out, flat):
    row_count, col_count, tile, comps, slots = sizes
    me_row = lax.axis_index("row")
    me_col = lax.axis_index("col")
    quad = geometry.shape[2]
    for slot in range(row_count * slots):
        for axis in range(comps // quad):
            flat[pl.ds(slot * comps + axis * quad, quad), :] = geometry[slot, axis]
    piv = pivots[...]
    owner_row, owner_col, local, lanes = pivot_place(piv, tile, row_count, col_count)
    picked = select_dot(
        flat[...], chosen_where(lax.broadcasted_iota(jnp.int32, (tile, tile), 0) == lanes)
    )
    top = jnp.zeros((comps, tile), jnp.float32)
    chosen = jnp.zeros((comps, tile), jnp.float32)
    for owner in range(row_count):
        for s in range(slots):
            number = table[me_row, s, owner]
            rows = (owner * slots + s) * comps
            block = flat[pl.ds(rows, comps), :]
            out[owner, pl.ds(s * comps, comps), :] = block
            hit = (owner_col == me_col) & (owner_row == owner) & (2 * local == number)
            chosen = jnp.where(hit, picked[rows : rows + comps], chosen)
            if owner == 0:
                here = jnp.full((comps, tile), (number == 0) & (me_col == 0))
                top = jnp.where(here, block, top)
    for owner in range(row_count):
        out[owner, pl.ds(slots * comps, comps), :] = top
        out[owner, pl.ds((slots + 1) * comps, comps), :] = chosen


def entries(rows, columns):
    total = None
    for column in columns:
        partial = None
        for row in rows:
            along_x = row[0] - column[0]
            along_y = row[1] - column[1]
            along_z = row[2] - column[2]
            square = along_x * along_x + along_y * along_y + along_z * along_z
            spacing = 1.0 / lax.rsqrt(square)
            scale = 1.0 / (spacing + SOFT_TURNS)
            turn = spacing - jnp.round(spacing)
            v = turn * turn
            c = ((v + A2) * v + A1) * v + A0
            value = (c * (c * c - TRIPLE)) * scale * row[3]
            partial = value if partial is None else partial + value
        partial = partial * column[3]
        total = partial if total is None else total + partial
    return total


def centred(geometry):
    u = (geometry - 0.5) * TURNS
    squares = u * u
    norm = squares + pltpu.roll(squares, 6, 0) + pltpu.roll(squares, 4, 0)
    return three_parts(u), three_parts(norm)


def left_features(geometry):
    parts, norms = centred(geometry)
    row = lax.broadcasted_iota(jnp.int32, geometry.shape, 0)
    stacked = jnp.where(
        row < 2,
        norms[0],
        jnp.where(
            row < 4,
            pltpu.roll(norms[1], 2, 0),
            jnp.where(row < 6, pltpu.roll(norms[2], 4, 0), 0.0),
        ),
    )
    blocks = [parts[i] for i in range(3) for _ in range(3)] + [stacked, jnp.ones_like(stacked), jnp.zeros_like(stacked)]
    return jnp.transpose(jnp.concatenate(blocks, axis=0)).astype(jnp.bfloat16)


def right_features(geometry, a, b):
    parts, norms = centred(geometry)
    row = lax.broadcasted_iota(jnp.int32, geometry.shape, 0)
    wanted = (row < 6) & ((row & 1) == a)
    turned = [part if a == b else pltpu.roll(part, (a - b) % 8, 0) for part in parts]
    doubled = [jnp.where(wanted, -2.0 * part, 0.0) for part in turned]
    ones = jnp.where(wanted, 1.0, 0.0)
    placed = jnp.zeros_like(ones)
    for i, norm in enumerate(norms):
        placed = jnp.where(row == i, pltpu.roll(norm, (i - b) % 8, 0) if i != b else norm, placed)
    blocks = [doubled[j] for _ in range(3) for j in range(3)] + [ones, placed, jnp.zeros_like(ones)]
    return jnp.concatenate(blocks, axis=0).astype(jnp.bfloat16)


def quick_entries(square, weights, column_weights, quad):
    total = None
    for b in range(quad):
        partial = None
        for a in range(quad):
            near = square(a, b)
            spacing = near * lax.rsqrt(near)
            scale = 1.0 / (spacing + SOFT_TURNS)
            turn = spacing - jnp.round(spacing)
            v = turn * turn
            c = ((v + A2) * v + A1) * v + A0
            value = (c * (c * c - TRIPLE)) * scale * weights[a]
            partial = value if partial is None else partial + value
        partial = partial * column_weights[b]
        total = partial if total is None else total + partial
    return total


def quick_fill(squares, points, base, columns, chunks, target, target_base, quad, height):
    found = []
    count = columns.shape[1]
    for group in range(height // 8):
        if group * 8 % PART == 0:
            nearest = None
        block = points[pl.ds(base + group * 8, 8), :]
        weights = [
            jnp.broadcast_to(block[:, 3 * quad + a : 3 * quad + a + 1], (8, 128)) for a in range(quad)
        ]
        for place, chunk in enumerate(chunks):
            loaded = {}
            for a in range(quad):
                for b in range(quad):
                    lane = ((a * quad + b) * count + chunk) * 128
                    value = squares[pl.ds(group * 8, 8), pl.ds(lane, 128)]
                    loaded[a, b] = value
                    nearest = value if nearest is None else jnp.minimum(nearest, value)
            target[pl.ds(target_base + group * 8, 8), pl.ds(place * 128, 128)] = quick_entries(
                lambda a, b: loaded[a, b], weights, [columns[3 * quad + b, chunk] for b in range(quad)], quad
            )
        if (group + 1) * 8 % PART == 0:
            found.append(jnp.where(jnp.min(nearest) < NEAR, 1, 0))
    return found


def fill(points, base, columns, chunks, target, target_base, quad, height):
    for group in range(height // 8):
        block = points[pl.ds(base + group * 8, 8), :]
        rows = [
            [
                jnp.broadcast_to(block[:, axis * quad + a : axis * quad + a + 1], (8, 128))
                for axis in range(4)
            ]
            for a in range(quad)
        ]
        for place, chunk in enumerate(chunks):
            cols = [[columns[axis * quad + b, chunk] for axis in range(4)] for b in range(quad)]
            target[pl.ds(target_base + group * 8, 8), pl.ds(place * 128, 128)] = entries(rows, cols)


def order_kernel(pivots, column_geometry, order, columns, right, column_points):
    quad = column_geometry.shape[1]
    tile = pivots.shape[1]
    lane_chunks = tile // 128
    for axis in range(4):
        column_points[pl.ds(axis * quad, quad), :] = column_geometry[axis]
    for a in range(quad):
        for b in range(quad):
            right[:, pl.ds((a * quad + b) * 2 * tile, 2 * tile)] = right_features(
                column_points[...], a, b
            )
    for axis in range(4):
        for b in range(quad):
            for chunk in range(2 * lane_chunks):
                part = column_geometry[axis, pl.ds(b, 1), pl.ds(chunk * 128, 128)]
                if axis < 3:
                    part = part * TURNS
                columns[axis * quad + b, chunk] = jnp.broadcast_to(part, (8, 128))
    piv = pivots[...]
    piv_col = as_column(piv)
    down = lax.broadcasted_iota(jnp.int32, (tile, tile), 0)
    across = lax.broadcasted_iota(jnp.int32, (tile, tile), 1)
    same = piv_col == piv
    earlier = down < across
    line = lax.broadcasted_iota(jnp.int32, (1, tile), 1)
    before = jnp.max(jnp.where(same & earlier, down, -1), axis=0, keepdims=True)
    after = jnp.max(jnp.where(same & (down > across), 1, 0), axis=0, keepdims=True)
    parent = jnp.max(jnp.where((piv_col == across) & earlier, down, -1), axis=0, keepdims=True)
    moved = jnp.max(parent)
    root = jnp.where(parent >= 0, parent, line)

    def doubled(carry):
        _, now = carry
        new = select_dot(jnp.broadcast_to(now, (8, tile)).astype(jnp.float32), chosen_where(down == now))
        new = new[:1].astype(jnp.int32)
        return jnp.max(jnp.where(new != now, 1, 0)), new

    _, root = lax.while_loop(lambda carry: carry[0] > 0, doubled, (jnp.where(moved >= 0, 1, 0), root))
    order[...] = jnp.concatenate([root, before, after] + [root] * 5, axis=0)


def main_kernel(
    sizes, arrived, shared, passed, table, pivots, order, columns, right, lower_inv, upper_inv,
    slab, upper_block, owned, points, filled, right_high, right_low, left, *squares,
):
    row_count, col_count, tile, comps, slots = sizes
    quad = 2 * comps // 8
    me_row = lax.axis_index("row")
    me_col = lax.axis_index("col")
    t = pl.program_id(0)
    tile_rows = pl.num_programs(0)
    lane_chunks = tile // 128
    height = HEIGHT
    steps = tile // height
    everything = range(2 * lane_chunks)

    def distances(block, buffer):
        rows = left[pl.ds(pl.multiple_of(block * height, height), height), :]
        buffer[...] = jnp.dot(rows, right[...], preferred_element_type=jnp.float32)

    def sweep(tile_index, chunks, last):
        def again(index, part):
            base = pl.multiple_of(index * height + part * PART, PART)
            fill(points.at[tile_index], base, columns, chunks, filled, base, quad, PART)

        def checked(index, near):
            total = functools.reduce(jnp.add, near)

            @pl.when(total > 0)
            def _():
                for place, flag in enumerate(near):

                    @pl.when(flag > 0)
                    def _():
                        again(index + place // (height // PART), place % (height // PART))

        def step(pair, near):
            index = 2 * pair
            checked(index - 2, near)
            flat = tile_index * steps + index
            found = []
            for part, (ahead, here) in enumerate(((squares[1], squares[0]), (squares[0], squares[1]))):
                distances(jnp.minimum(flat + 1 + part, last), ahead)
                base = pl.multiple_of((index + part) * height, height)
                found.extend(
                    quick_fill(
                        here, points.at[tile_index], base, columns, chunks, filled, base, quad, height
                    )
                )
            return tuple(found)

        checked(steps - 2, lax.fori_loop(0, steps // 2, step, (0,) * (2 * height // PART)))

    @pl.when(t == 0)
    def _():
        for source in range(row_count):
            for s in range(slots):
                number = table[source, s, me_row]

                @pl.when(number & 1 == 0)
                def _():
                    owned[lax.shift_right_logical(number, 1)] = arrived[source, pl.ds(s * comps, comps), :]

        piv = pivots[...]
        owner_row, owner_col, local, lanes = pivot_place(piv, tile, row_count, col_count)
        down = lax.broadcasted_iota(jnp.int32, (tile, tile), 0)
        across = lax.broadcasted_iota(jnp.int32, (tile, tile), 1)
        root = order[pl.ds(0, 1), :]
        before = order[pl.ds(1, 1), :]
        after = order[pl.ds(2, 1), :]
        top = shared[pl.ds(0, comps), :] + passed[pl.ds(0, comps), :]
        chosen = shared[pl.ds(comps, comps), :] + passed[pl.ds(comps, comps), :]
        carried = select_dot(top, chosen_where(down == root))
        again = select_dot(carried, chosen_where(down == before))
        new_top = jnp.where(before >= 0, again, chosen)
        mine = (owner_row == me_row) & (owner_col == me_col) & (after == 0) & (piv >= tile)
        lane_col = as_column(lanes)
        place = chosen_where(lane_col == across)
        parts = []
        for k in range(owned.shape[0]):
            parts.append(jnp.where(mine & (local == k), carried, 0.0))
        marks = []
        for k in range(owned.shape[0]):
            marks.append(jnp.broadcast_to(jnp.where(mine & (local == k), 1.0, 0.0), (comps, tile)))
        sent = select_dot(jnp.concatenate(parts, axis=0), place)
        landed = jnp.dot(
            jnp.concatenate(marks, axis=0).astype(jnp.bfloat16), place, preferred_element_type=jnp.float32
        )
        factor = jnp.where(
            lax.broadcasted_iota(jnp.int32, (comps, tile), 0) < 3 * quad, TURNS, WEIGHT
        )
        leading = jnp.full((comps, tile), (me_row == 0) & (me_col == 0))
        count = owned.shape[0]
        for k in range(count):
            fresh = sent[k * comps : (k + 1) * comps]
            hit = landed[k * comps : (k + 1) * comps] > 0.5
            mixed = jnp.where(hit, fresh, owned[k])
            if k == 0:
                mixed = jnp.where(leading, new_top, mixed)
            points[k] = jnp.transpose(mixed * factor)
            left[pl.ds(k * tile, tile), :] = left_features(mixed)
        points[count] = jnp.transpose(new_top * factor)
        left[pl.ds(count * tile, tile), :] = left_features(new_top)
        distances(count * steps, squares[0])
        sweep(count, range(lane_chunks, 2 * lane_chunks), count * steps + steps - 1)
        distances(0, squares[0])
        upper = split_dot(lower_inv[...], filled[:, :tile])
        upper_block[...] = upper
        both = jnp.concatenate([upper_inv[...], -split_dot(upper_inv[...], upper)], axis=1)
        right_high[...], right_low[...] = two_parts(both)

    sweep(t, everything, tile_rows * steps - 1)
    high, low = two_parts(filled[:, :tile])
    dot = functools.partial(jnp.dot, preferred_element_type=jnp.float32)
    product = dot(high, right_low[...]) + dot(low, right_high[...]) + dot(high, right_high[...])
    slab[:, :tile] = product[:, :tile]
    slab[:, tile:] = product[:, tile:] + filled[:, tile:]


def per_device(row_geometry, column_geometry, octree_slot, pivots, lower_inv, upper_inv):
    row_count = lax.axis_size("row")
    col_count = lax.axis_size("col")
    tile = pivots.shape[0]
    slots_all, axes, quad = row_geometry.shape[2:5]
    slots = slots_all // row_count
    tile_rows = slots_all // 2
    comps = axes * quad
    sizes = (row_count, col_count, tile, comps, slots)
    geometry = row_geometry[0, 0]
    table = jnp.swapaxes(octree_slot[0], 1, 2)
    pivot_row = pivots.reshape(1, tile)
    vmem = pl.BlockSpec(memory_space=pltpu.VMEM)
    smem = pl.BlockSpec(memory_space=pltpu.SMEM)
    depth = (slots + 2) * comps
    packed = pl.pallas_call(
        functools.partial(pack_kernel, sizes),
        out_shape=pltpu.VMEM((row_count, depth, tile), jnp.float32),
        in_specs=[vmem, smem, vmem],
        out_specs=vmem,
        scratch_shapes=[pltpu.VMEM((slots_all * comps, tile), jnp.float32)],
        name="pack",
    )(geometry, table, pivot_row)
    arrived = lax.all_to_all(packed, "row", 0, 0, tiled=True)
    shared = jnp.sum(arrived[:, slots * comps :, :], axis=0)
    passed = jnp.zeros_like(shared)
    step = 1
    while step < col_count:
        partner = [(j, j ^ step) for j in range(col_count)]
        passed = lax.ppermute(shared, "col", partner)
        step *= 2
        if step < col_count:
            shared = shared + passed
    passed = pltpu.with_memory_space_constraint(passed, pltpu.VMEM)
    shared = pltpu.with_memory_space_constraint(shared, pltpu.VMEM)
    arrived = pltpu.with_memory_space_constraint(arrived, pltpu.VMEM)
    order, columns, right = pl.pallas_call(
        order_kernel,
        out_shape=(
            pltpu.VMEM((8, tile), jnp.int32),
            pltpu.VMEM((comps, 2 * tile // 128, 8, 128), jnp.float32),
            pltpu.VMEM((12 * comps, quad * quad * 2 * tile), jnp.bfloat16),
        ),
        in_specs=[vmem, vmem],
        out_specs=(vmem, vmem, vmem),
        scratch_shapes=[pltpu.VMEM((comps, 2 * tile), jnp.float32)],
        name="order",
    )(pivot_row, column_geometry)
    order, columns, right = (
        pltpu.with_memory_space_constraint(part, pltpu.VMEM) for part in (order, columns, right)
    )
    slab, upper_block = pl.pallas_call(
        functools.partial(main_kernel, sizes),
        grid=(tile_rows,),
        out_shape=(
            jax.ShapeDtypeStruct((tile_rows * tile, 2 * tile), jnp.float32),
            jax.ShapeDtypeStruct((tile, tile), jnp.float32),
        ),
        in_specs=[vmem, vmem, vmem, smem, vmem, vmem, vmem, vmem, vmem, vmem],
        out_specs=(
            pl.BlockSpec((tile, 2 * tile), lambda t: (t, 0)),
            pl.BlockSpec((tile, tile), lambda t: (0, 0)),
        ),
        scratch_shapes=[
            pltpu.VMEM((tile_rows, comps, tile), jnp.float32),
            pltpu.VMEM((tile_rows + 1, tile, comps), jnp.float32),
            pltpu.VMEM((tile, 2 * tile), jnp.float32),
            pltpu.VMEM((tile, 2 * tile), jnp.bfloat16),
            pltpu.VMEM((tile, 2 * tile), jnp.bfloat16),
            pltpu.VMEM(((tile_rows + 1) * tile, 12 * comps), jnp.bfloat16),
            pltpu.VMEM((HEIGHT, quad * quad * 2 * tile), jnp.float32),
            pltpu.VMEM((HEIGHT, quad * quad * 2 * tile), jnp.float32),
        ],
        name="panel",
        compiler_params=pltpu.CompilerParams(),
    )(arrived, shared, passed, table, pivot_row, order, columns, right, lower_inv, upper_inv)
    return (slab.reshape(1, 1, tile_rows, tile, 2 * tile), upper_block)


def solution(mesh):
    placed = (
        P("col", "row", None, None, None, None),
        P(),
        P("col", None, None, None),
        P(),
        P(),
        P(),
    )
    return jax.shard_map(
        per_device,
        mesh=mesh,
        in_specs=placed,
        out_specs=(P("row", "col", None, None, None), P()),
        check_vma=False,
    )
```

```python
import functools
import math

import jax
import jax.numpy as jnp
from jax import lax
from jax.experimental import pallas as pl
from jax.experimental.pallas import tpu as pltpu
from jax.sharding import PartitionSpec as P

KAPPA = 9.0
SOFTEN = 0.05

FIT = (1.99999988, -4.38646535, 1.60268206, -0.22763882)
LEAD = FIT[3]
A0, A1, A2 = FIT[0] / LEAD, FIT[1] / LEAD, FIT[2] / LEAD
TRIPLE = 3.0 / (LEAD * LEAD)
TURNS = KAPPA / (2.0 * math.pi)
SOFT_TURNS = SOFTEN * TURNS
WEIGHT = 0.5 * LEAD**3 * TURNS
NEAR = (0.003 * TURNS) ** 2
PART = 16
HEIGHT = 64


def split(value, divisor):
    if divisor & (divisor - 1) == 0:
        shift = divisor.bit_length() - 1
        return lax.shift_right_logical(value, shift), value & (divisor - 1)
    return lax.div(value, divisor), lax.rem(value, divisor)


def as_column(row):
    count = row.shape[1]
    return jnp.transpose(jnp.broadcast_to(row, (8, count)))[:, :1]


def three_parts(value):
    parts = []
    for _ in range(3):
        part = value.astype(jnp.bfloat16).astype(jnp.float32)
        parts.append(part)
        value = value - part
    return parts


def select_dot(values, choice):
    count = values.shape[0]
    stacked = jnp.concatenate(three_parts(values), axis=0).astype(jnp.bfloat16)
    product = jnp.dot(stacked, choice, preferred_element_type=jnp.float32)
    return product[:count] + product[count : 2 * count] + product[2 * count :]


def split_dot(left, right):
    dot = functools.partial(jnp.dot, preferred_element_type=jnp.float32)
    return dot(left[0], right[1]) + dot(left[1], right[0]) + dot(left[0], right[0])


def two_parts(value):
    high = value.astype(jnp.bfloat16)
    return high, (value - high.astype(jnp.float32)).astype(jnp.bfloat16)


def chosen_where(mask):
    return jnp.where(mask, 1.0, 0.0).astype(jnp.bfloat16)


def pivot_place(pivots, tile, row_count, col_count):
    tiles, lanes = split(pivots, tile)
    rest, owner_row = split(tiles, row_count)
    local, owner_col = split(rest, col_count)
    return owner_row, owner_col, local, lanes


def pack_kernel(sizes, geometry, table, pivots, out, flat):
    row_count, col_count, tile, comps, slots = sizes
    me_row = lax.axis_index("row")
    me_col = lax.axis_index("col")
    quad = geometry.shape[2]
    for slot in range(row_count * slots):
        for axis in range(comps // quad):
            flat[pl.ds(slot * comps + axis * quad, quad), :] = geometry[slot, axis]
    piv = pivots[...]
    owner_row, owner_col, local, lanes = pivot_place(piv, tile, row_count, col_count)
    picked = select_dot(
        flat[...], chosen_where(lax.broadcasted_iota(jnp.int32, (tile, tile), 0) == lanes)
    )
    top = jnp.zeros((comps, tile), jnp.float32)
    chosen = jnp.zeros((comps, tile), jnp.float32)
    for owner in range(row_count):
        for s in range(slots):
            number = table[me_row, s, owner]
            rows = (owner * slots + s) * comps
            block = flat[pl.ds(rows, comps), :]
            out[owner, pl.ds(s * comps, comps), :] = block
            hit = (owner_col == me_col) & (owner_row == owner) & (2 * local == number)
            chosen = jnp.where(hit, picked[rows : rows + comps], chosen)
            if owner == 0:
                here = jnp.full((comps, tile), (number == 0) & (me_col == 0))
                top = jnp.where(here, block, top)
    for owner in range(row_count):
        out[owner, pl.ds(slots * comps, comps), :] = top
        out[owner, pl.ds((slots + 1) * comps, comps), :] = chosen


def entries(rows, columns):
    total = None
    for column in columns:
        partial = None
        for row in rows:
            along_x = row[0] - column[0]
            along_y = row[1] - column[1]
            along_z = row[2] - column[2]
            square = along_x * along_x + along_y * along_y + along_z * along_z
            spacing = 1.0 / lax.rsqrt(square)
            scale = 1.0 / (spacing + SOFT_TURNS)
            turn = spacing - jnp.round(spacing)
            v = turn * turn
            c = ((v + A2) * v + A1) * v + A0
            value = (c * (c * c - TRIPLE)) * scale * row[3]
            partial = value if partial is None else partial + value
        partial = partial * column[3]
        total = partial if total is None else total + partial
    return total


def centred(geometry):
    u = (geometry - 0.5) * TURNS
    squares = u * u
    norm = squares + pltpu.roll(squares, 6, 0) + pltpu.roll(squares, 4, 0)
    return three_parts(u), three_parts(norm)


def left_features(geometry):
    parts, norms = centred(geometry)
    row = lax.broadcasted_iota(jnp.int32, geometry.shape, 0)
    stacked = jnp.where(
        row < 2,
        norms[0],
        jnp.where(
            row < 4,
            pltpu.roll(norms[1], 2, 0),
            jnp.where(row < 6, pltpu.roll(norms[2], 4, 0), 0.0),
        ),
    )
    blocks = [parts[i] for i in range(3) for _ in range(3)] + [stacked, jnp.ones_like(stacked), jnp.zeros_like(stacked)]
    return jnp.transpose(jnp.concatenate(blocks, axis=0)).astype(jnp.bfloat16)


def right_features(geometry, a, b):
    parts, norms = centred(geometry)
    row = lax.broadcasted_iota(jnp.int32, geometry.shape, 0)
    wanted = (row < 6) & ((row & 1) == a)
    turned = [part if a == b else pltpu.roll(part, (a - b) % 8, 0) for part in parts]
    doubled = [jnp.where(wanted, -2.0 * part, 0.0) for part in turned]
    ones = jnp.where(wanted, 1.0, 0.0)
    placed = jnp.zeros_like(ones)
    for i, norm in enumerate(norms):
        placed = jnp.where(row == i, pltpu.roll(norm, (i - b) % 8, 0) if i != b else norm, placed)
    blocks = [doubled[j] for _ in range(3) for j in range(3)] + [ones, placed, jnp.zeros_like(ones)]
    return jnp.concatenate(blocks, axis=0).astype(jnp.bfloat16)


def quick_entries(square, weights, column_weights, quad):
    total = None
    for b in range(quad):
        partial = None
        for a in range(quad):
            near = square(a, b)
            spacing = near * lax.rsqrt(near)
            scale = 1.0 / (spacing + SOFT_TURNS)
            turn = spacing - jnp.round(spacing)
            v = turn * turn
            c = ((v + A2) * v + A1) * v + A0
            value = (c * (c * c - TRIPLE)) * scale * weights[a]
            partial = value if partial is None else partial + value
        partial = partial * column_weights[b]
        total = partial if total is None else total + partial
    return total


def quick_fill(squares, points, base, columns, chunks, target, target_base, quad, height):
    found = []
    count = columns.shape[1]
    for group in range(height // 8):
        if group * 8 % PART == 0:
            nearest = None
        block = points[pl.ds(base + group * 8, 8), :]
        weights = [
            jnp.broadcast_to(block[:, 3 * quad + a : 3 * quad + a + 1], (8, 128)) for a in range(quad)
        ]
        for place, chunk in enumerate(chunks):
            loaded = {}
            for a in range(quad):
                for b in range(quad):
                    lane = ((a * quad + b) * count + chunk) * 128
                    value = squares[pl.ds(group * 8, 8), pl.ds(lane, 128)]
                    loaded[a, b] = value
                    nearest = value if nearest is None else jnp.minimum(nearest, value)
            target[pl.ds(target_base + group * 8, 8), pl.ds(place * 128, 128)] = quick_entries(
                lambda a, b: loaded[a, b], weights, [columns[3 * quad + b, chunk] for b in range(quad)], quad
            )
        if (group + 1) * 8 % PART == 0:
            found.append(jnp.where(jnp.min(nearest) < NEAR, 1, 0))
    return found


def fill(points, base, columns, chunks, target, target_base, quad, height):
    for group in range(height // 8):
        block = points[pl.ds(base + group * 8, 8), :]
        rows = [
            [
                jnp.broadcast_to(block[:, axis * quad + a : axis * quad + a + 1], (8, 128))
                for axis in range(4)
            ]
            for a in range(quad)
        ]
        for place, chunk in enumerate(chunks):
            cols = [[columns[axis * quad + b, chunk] for axis in range(4)] for b in range(quad)]
            target[pl.ds(target_base + group * 8, 8), pl.ds(place * 128, 128)] = entries(rows, cols)


def order_kernel(
    sizes, pivots, column_geometry, columns, right, picks_root, picks_before, places, marks, landed, column_points
):
    row_count, col_count, tile, comps, slots = sizes
    quad = column_geometry.shape[1]
    lane_chunks = tile // 128
    for axis in range(4):
        column_points[pl.ds(axis * quad, quad), :] = column_geometry[axis]
    for a in range(quad):
        for b in range(quad):
            right[:, pl.ds((a * quad + b) * 2 * tile, 2 * tile)] = right_features(
                column_points[...], a, b
            )
    for axis in range(4):
        for b in range(quad):
            for chunk in range(2 * lane_chunks):
                part = column_geometry[axis, pl.ds(b, 1), pl.ds(chunk * 128, 128)]
                if axis < 3:
                    part = part * TURNS
                columns[axis * quad + b, chunk] = jnp.broadcast_to(part, (8, 128))
    piv = pivots[...]
    piv_col = as_column(piv)
    down = lax.broadcasted_iota(jnp.int32, (tile, tile), 0)
    across = lax.broadcasted_iota(jnp.int32, (tile, tile), 1)
    same = piv_col == piv
    earlier = down < across
    line = lax.broadcasted_iota(jnp.int32, (1, tile), 1)
    before = jnp.max(jnp.where(same & earlier, down, -1), axis=0, keepdims=True)
    after = jnp.max(jnp.where(same & (down > across), 1, 0), axis=0, keepdims=True)
    parent = jnp.max(jnp.where((piv_col == across) & earlier, down, -1), axis=0, keepdims=True)
    moved = jnp.max(parent)
    root = jnp.where(parent >= 0, parent, line)

    def doubled(carry):
        _, now = carry
        new = select_dot(jnp.broadcast_to(now, (8, tile)).astype(jnp.float32), chosen_where(down == now))
        new = new[:1].astype(jnp.int32)
        return jnp.max(jnp.where(new != now, 1, 0)), new

    _, root = lax.while_loop(lambda carry: carry[0] > 0, doubled, (jnp.where(moved >= 0, 1, 0), root))
    picks_root[...] = chosen_where(down == root)
    picks_before[...] = chosen_where(down == before)
    owner_row, owner_col, local, lanes = pivot_place(piv, tile, row_count, col_count)
    mine = (owner_row == lax.axis_index("row")) & (owner_col == lax.axis_index("col"))
    mine = mine & (after == 0) & (piv >= tile)
    place = chosen_where(as_column(lanes) == across)
    places[...] = place
    count = landed.shape[0]
    rows = [jnp.broadcast_to(jnp.where(mine & (local == k), 1.0, 0.0), (comps, tile)) for k in range(count)]
    rows.append(jnp.broadcast_to(jnp.where(before >= 0, 1.0, 0.0), (comps, tile)))
    for k, row in enumerate(rows):
        marks[k] = row
    hits = jnp.dot(
        jnp.concatenate(rows[:count], axis=0).astype(jnp.bfloat16), place, preferred_element_type=jnp.float32
    )
    for k in range(count):
        landed[k] = hits[k * comps : (k + 1) * comps]


def early_kernel(sizes, arrived, table, lower_inv, upper_inv, owned, lower, upper):
    row_count, col_count, tile, comps, slots = sizes
    me_row = lax.axis_index("row")
    for source in range(row_count):
        for s in range(slots):
            number = table[source, s, me_row]

            @pl.when(number & 1 == 0)
            def _():
                owned[lax.shift_right_logical(number, 1)] = arrived[source, pl.ds(s * comps, comps), :]

    lower[0], lower[1] = two_parts(lower_inv[...])
    upper[0], upper[1] = two_parts(upper_inv[...])


def main_kernel(
    sizes, owned, shared, passed, columns, right, picks_root, picks_before, places, marks, landed, lower, upper,
    slab, upper_block, points, filled, right_high, right_low, left, *squares,
):
    row_count, col_count, tile, comps, slots = sizes
    quad = 2 * comps // 8
    me_row = lax.axis_index("row")
    me_col = lax.axis_index("col")
    t = pl.program_id(0)
    tile_rows = pl.num_programs(0)
    lane_chunks = tile // 128
    height = HEIGHT
    steps = tile // height
    everything = range(2 * lane_chunks)

    def distances(block, buffer):
        rows = left[pl.ds(pl.multiple_of(block * height, height), height), :]
        buffer[...] = jnp.dot(rows, right[...], preferred_element_type=jnp.float32)

    def sweep(tile_index, chunks, last):
        def again(index, part):
            base = pl.multiple_of(index * height + part * PART, PART)
            fill(points.at[tile_index], base, columns, chunks, filled, base, quad, PART)

        def checked(index, near):
            total = functools.reduce(jnp.add, near)

            @pl.when(total > 0)
            def _():
                for place, flag in enumerate(near):

                    @pl.when(flag > 0)
                    def _():
                        again(index + place // (height // PART), place % (height // PART))

        def step(pair, near):
            index = 2 * pair
            checked(index - 2, near)
            flat = tile_index * steps + index
            found = []
            for part, (ahead, here) in enumerate(((squares[1], squares[0]), (squares[0], squares[1]))):
                distances(jnp.minimum(flat + 1 + part, last), ahead)
                base = pl.multiple_of((index + part) * height, height)
                found.extend(
                    quick_fill(
                        here, points.at[tile_index], base, columns, chunks, filled, base, quad, height
                    )
                )
            return tuple(found)

        checked(steps - 2, lax.fori_loop(0, steps // 2, step, (0,) * (2 * height // PART)))

    @pl.when(t == 0)
    def _():
        top = shared[pl.ds(0, comps), :] + passed[pl.ds(0, comps), :]
        chosen = shared[pl.ds(comps, comps), :] + passed[pl.ds(comps, comps), :]
        count = owned.shape[0]
        carried = select_dot(top, picks_root[...])
        again = select_dot(carried, picks_before[...])
        new_top = jnp.where(marks[count] > 0.5, again, chosen)
        sent = select_dot(
            jnp.concatenate([marks[k] * carried for k in range(count)], axis=0), places[...]
        )
        factor = jnp.where(
            lax.broadcasted_iota(jnp.int32, (comps, tile), 0) < 3 * quad, TURNS, WEIGHT
        )
        leading = jnp.full((comps, tile), (me_row == 0) & (me_col == 0))
        for k in range(count):
            fresh = sent[k * comps : (k + 1) * comps]
            hit = landed[k] > 0.5
            mixed = jnp.where(hit, fresh, owned[k])
            if k == 0:
                mixed = jnp.where(leading, new_top, mixed)
            points[k] = jnp.transpose(mixed * factor)
            left[pl.ds(k * tile, tile), :] = left_features(mixed)
        points[count] = jnp.transpose(new_top * factor)
        left[pl.ds(count * tile, tile), :] = left_features(new_top)
        distances(count * steps, squares[0])
        sweep(count, range(lane_chunks, 2 * lane_chunks), count * steps + steps - 1)
        distances(0, squares[0])
        solved = split_dot((lower[0], lower[1]), two_parts(filled[:, :tile]))
        upper_block[...] = solved
        high, low = two_parts(-split_dot((upper[0], upper[1]), two_parts(solved)))
        right_high[:, :tile], right_high[:, tile:] = upper[0], high
        right_low[:, :tile], right_low[:, tile:] = upper[1], low

    sweep(t, everything, tile_rows * steps - 1)
    high, low = two_parts(filled[:, :tile])
    dot = functools.partial(jnp.dot, preferred_element_type=jnp.float32)
    product = dot(high, right_low[...]) + dot(low, right_high[...]) + dot(high, right_high[...])
    slab[:, :tile] = product[:, :tile]
    slab[:, tile:] = product[:, tile:] + filled[:, tile:]


def per_device(row_geometry, column_geometry, octree_slot, pivots, lower_inv, upper_inv):
    row_count = lax.axis_size("row")
    col_count = lax.axis_size("col")
    tile = pivots.shape[0]
    slots_all, axes, quad = row_geometry.shape[2:5]
    slots = slots_all // row_count
    tile_rows = slots_all // 2
    comps = axes * quad
    sizes = (row_count, col_count, tile, comps, slots)
    geometry = row_geometry[0, 0]
    table = jnp.swapaxes(octree_slot[0], 1, 2)
    pivot_row = pivots.reshape(1, tile)
    vmem = pl.BlockSpec(memory_space=pltpu.VMEM)
    smem = pl.BlockSpec(memory_space=pltpu.SMEM)
    depth = (slots + 2) * comps
    packed = pl.pallas_call(
        functools.partial(pack_kernel, sizes),
        out_shape=pltpu.VMEM((row_count, depth, tile), jnp.float32),
        in_specs=[vmem, smem, vmem],
        out_specs=vmem,
        scratch_shapes=[pltpu.VMEM((slots_all * comps, tile), jnp.float32)],
        name="pack",
    )(geometry, table, pivot_row)
    arrived = lax.all_to_all(packed, "row", 0, 0, tiled=True)
    shared = jnp.sum(arrived[:, slots * comps :, :], axis=0)
    keep = functools.partial(pltpu.with_memory_space_constraint, memory_space=pltpu.VMEM)
    ready = pl.pallas_call(
        functools.partial(early_kernel, sizes),
        out_shape=(
            pltpu.VMEM((tile_rows, comps, tile), jnp.float32),
            pltpu.VMEM((2, tile, tile), jnp.bfloat16),
            pltpu.VMEM((2, tile, tile), jnp.bfloat16),
        ),
        in_specs=[vmem, smem, vmem, vmem],
        out_specs=(vmem,) * 3,
        name="early",
    )(keep(arrived), table, lower_inv, upper_inv)
    passed = jnp.zeros_like(shared)
    step = 1
    while step < col_count:
        partner = [(j, j ^ step) for j in range(col_count)]
        passed = lax.ppermute(shared, "col", partner)
        step *= 2
        if step < col_count:
            shared = shared + passed
            shared, ready = lax.optimization_barrier((shared, ready))
    order = pl.pallas_call(
        functools.partial(order_kernel, sizes),
        out_shape=(
            pltpu.VMEM((comps, 2 * tile // 128, 8, 128), jnp.float32),
            pltpu.VMEM((12 * comps, quad * quad * 2 * tile), jnp.bfloat16),
            pltpu.VMEM((tile, tile), jnp.bfloat16),
            pltpu.VMEM((tile, tile), jnp.bfloat16),
            pltpu.VMEM((tile, tile), jnp.bfloat16),
            pltpu.VMEM((tile_rows + 1, comps, tile), jnp.float32),
            pltpu.VMEM((tile_rows, comps, tile), jnp.float32),
        ),
        in_specs=[vmem, vmem],
        out_specs=(vmem,) * 7,
        scratch_shapes=[pltpu.VMEM((comps, 2 * tile), jnp.float32)],
        name="order",
    )(pivot_row, column_geometry)
    owned, lower, upper = map(keep, ready)
    slab, upper_block = pl.pallas_call(
        functools.partial(main_kernel, sizes),
        grid=(tile_rows,),
        out_shape=(
            jax.ShapeDtypeStruct((tile_rows * tile, 2 * tile), jnp.float32),
            jax.ShapeDtypeStruct((tile, tile), jnp.float32),
        ),
        in_specs=[vmem] * 12,
        out_specs=(
            pl.BlockSpec((tile, 2 * tile), lambda t: (t, 0)),
            pl.BlockSpec((tile, tile), lambda t: (0, 0)),
        ),
        scratch_shapes=[
            pltpu.VMEM((tile_rows + 1, tile, comps), jnp.float32),
            pltpu.VMEM((tile, 2 * tile), jnp.float32),
            pltpu.VMEM((tile, 2 * tile), jnp.bfloat16),
            pltpu.VMEM((tile, 2 * tile), jnp.bfloat16),
            pltpu.VMEM(((tile_rows + 1) * tile, 12 * comps), jnp.bfloat16),
            pltpu.VMEM((HEIGHT, quad * quad * 2 * tile), jnp.float32),
            pltpu.VMEM((HEIGHT, quad * quad * 2 * tile), jnp.float32),
        ],
        name="panel",
        compiler_params=pltpu.CompilerParams(),
    )(owned, keep(shared), keep(passed), *map(keep, order), lower, upper)
    return (slab.reshape(1, 1, tile_rows, tile, 2 * tile), upper_block)


def solution(mesh):
    placed = (
        P("col", "row", None, None, None, None),
        P(),
        P("col", None, None, None),
        P(),
        P(),
        P(),
    )
    return jax.shard_map(
        per_device,
        mesh=mesh,
        in_specs=placed,
        out_specs=(P("row", "col", None, None, None), P()),
        check_vma=False,
    )
```

```python
import functools
import math

import jax
import jax.numpy as jnp
from jax import lax
from jax.experimental import pallas as pl
from jax.experimental.pallas import tpu as pltpu
from jax.sharding import PartitionSpec as P

KAPPA = 9.0
SOFTEN = 0.05

FIT = (1.99999988, -4.38646535, 1.60268206, -0.22763882)
LEAD = FIT[3]
A0, A1, A2 = FIT[0] / LEAD, FIT[1] / LEAD, FIT[2] / LEAD
TRIPLE = 3.0 / (LEAD * LEAD)
TURNS = KAPPA / (2.0 * math.pi)
SOFT_TURNS = SOFTEN * TURNS
WEIGHT = 0.5 * LEAD**3 * TURNS
NEAR = (0.003 * TURNS) ** 2
PART = 16
HEIGHT = 64


def split(value, divisor):
    if divisor & (divisor - 1) == 0:
        shift = divisor.bit_length() - 1
        return lax.shift_right_logical(value, shift), value & (divisor - 1)
    return lax.div(value, divisor), lax.rem(value, divisor)


def as_column(row):
    count = row.shape[1]
    return jnp.transpose(jnp.broadcast_to(row, (8, count)))[:, :1]


def three_parts(value):
    parts = []
    for _ in range(3):
        part = value.astype(jnp.bfloat16).astype(jnp.float32)
        parts.append(part)
        value = value - part
    return parts


def select_dot(values, choice):
    count = values.shape[0]
    stacked = jnp.concatenate(three_parts(values), axis=0).astype(jnp.bfloat16)
    product = jnp.dot(stacked, choice, preferred_element_type=jnp.float32)
    return product[:count] + product[count : 2 * count] + product[2 * count :]


def split_dot(left, right):
    dot = functools.partial(jnp.dot, preferred_element_type=jnp.float32)
    return dot(left[0], right[1]) + dot(left[1], right[0]) + dot(left[0], right[0])


def two_parts(value):
    high = value.astype(jnp.bfloat16)
    return high, (value - high.astype(jnp.float32)).astype(jnp.bfloat16)


def chosen_where(mask):
    return jnp.where(mask, 1.0, 0.0).astype(jnp.bfloat16)


def pivot_place(pivots, tile, row_count, col_count):
    tiles, lanes = split(pivots, tile)
    rest, owner_row = split(tiles, row_count)
    local, owner_col = split(rest, col_count)
    return owner_row, owner_col, local, lanes


def pack_kernel(sizes, geometry, table, pivots, out, flat):
    row_count, col_count, tile, comps, slots = sizes
    me_row = lax.axis_index("row")
    me_col = lax.axis_index("col")
    quad = geometry.shape[2]
    for slot in range(row_count * slots):
        for axis in range(comps // quad):
            flat[pl.ds(slot * comps + axis * quad, quad), :] = geometry[slot, axis]
    piv = pivots[...]
    owner_row, owner_col, local, lanes = pivot_place(piv, tile, row_count, col_count)
    picked = select_dot(
        flat[...], chosen_where(lax.broadcasted_iota(jnp.int32, (tile, tile), 0) == lanes)
    )
    top = jnp.zeros((comps, tile), jnp.float32)
    chosen = jnp.zeros((comps, tile), jnp.float32)
    for owner in range(row_count):
        for s in range(slots):
            number = table[me_row, s, owner]
            rows = (owner * slots + s) * comps
            block = flat[pl.ds(rows, comps), :]
            out[owner, pl.ds(s * comps, comps), :] = block
            hit = (owner_col == me_col) & (owner_row == owner) & (2 * local == number)
            chosen = jnp.where(hit, picked[rows : rows + comps], chosen)
            if owner == 0:
                here = jnp.full((comps, tile), (number == 0) & (me_col == 0))
                top = jnp.where(here, block, top)
    for owner in range(row_count):
        out[owner, pl.ds(slots * comps, comps), :] = top
        out[owner, pl.ds((slots + 1) * comps, comps), :] = chosen


def entries(rows, columns):
    total = None
    for column in columns:
        partial = None
        for row in rows:
            along_x = row[0] - column[0]
            along_y = row[1] - column[1]
            along_z = row[2] - column[2]
            square = along_x * along_x + along_y * along_y + along_z * along_z
            spacing = 1.0 / lax.rsqrt(square)
            scale = 1.0 / (spacing + SOFT_TURNS)
            turn = spacing - jnp.round(spacing)
            v = turn * turn
            c = ((v + A2) * v + A1) * v + A0
            value = (c * (c * c - TRIPLE)) * scale * row[3]
            partial = value if partial is None else partial + value
        partial = partial * column[3]
        total = partial if total is None else total + partial
    return total


def centred(geometry):
    u = (geometry - 0.5) * TURNS
    squares = u * u
    norm = squares + pltpu.roll(squares, 6, 0) + pltpu.roll(squares, 4, 0)
    return three_parts(u), three_parts(norm)


def left_features(geometry):
    parts, norms = centred(geometry)
    row = lax.broadcasted_iota(jnp.int32, geometry.shape, 0)
    stacked = jnp.where(
        row < 2,
        norms[0],
        jnp.where(
            row < 4,
            pltpu.roll(norms[1], 2, 0),
            jnp.where(row < 6, pltpu.roll(norms[2], 4, 0), 0.0),
        ),
    )
    blocks = [parts[i] for i in range(3) for _ in range(3)] + [stacked, jnp.ones_like(stacked), jnp.zeros_like(stacked)]
    return jnp.transpose(jnp.concatenate(blocks, axis=0)).astype(jnp.bfloat16)


def right_features(geometry, a, b):
    parts, norms = centred(geometry)
    row = lax.broadcasted_iota(jnp.int32, geometry.shape, 0)
    wanted = (row < 6) & ((row & 1) == a)
    turned = [part if a == b else pltpu.roll(part, (a - b) % 8, 0) for part in parts]
    doubled = [jnp.where(wanted, -2.0 * part, 0.0) for part in turned]
    ones = jnp.where(wanted, 1.0, 0.0)
    placed = jnp.zeros_like(ones)
    for i, norm in enumerate(norms):
        placed = jnp.where(row == i, pltpu.roll(norm, (i - b) % 8, 0) if i != b else norm, placed)
    blocks = [doubled[j] for _ in range(3) for j in range(3)] + [ones, placed, jnp.zeros_like(ones)]
    return jnp.concatenate(blocks, axis=0).astype(jnp.bfloat16)


def quick_entries(square, weights, column_weights, quad):
    total = None
    for b in range(quad):
        partial = None
        for a in range(quad):
            near = square(a, b)
            spacing = near * lax.rsqrt(near)
            scale = 1.0 / (spacing + SOFT_TURNS)
            turn = spacing - jnp.round(spacing)
            v = turn * turn
            c = ((v + A2) * v + A1) * v + A0
            value = (c * (c * c - TRIPLE)) * scale * weights[a]
            partial = value if partial is None else partial + value
        partial = partial * column_weights[b]
        total = partial if total is None else total + partial
    return total


def quick_fill(squares, points, base, columns, chunks, target, target_base, quad, height):
    found = []
    count = columns.shape[1]
    for group in range(height // 8):
        if group * 8 % PART == 0:
            nearest = None
        block = points[pl.ds(base + group * 8, 8), :]
        weights = [
            jnp.broadcast_to(block[:, 3 * quad + a : 3 * quad + a + 1], (8, 128)) for a in range(quad)
        ]
        for place, chunk in enumerate(chunks):
            loaded = {}
            for a in range(quad):
                for b in range(quad):
                    lane = ((a * quad + b) * count + chunk) * 128
                    value = squares[pl.ds(group * 8, 8), pl.ds(lane, 128)]
                    loaded[a, b] = value
                    nearest = value if nearest is None else jnp.minimum(nearest, value)
            target[pl.ds(target_base + group * 8, 8), pl.ds(place * 128, 128)] = quick_entries(
                lambda a, b: loaded[a, b], weights, [columns[3 * quad + b, chunk] for b in range(quad)], quad
            )
        if (group + 1) * 8 % PART == 0:
            found.append(jnp.where(jnp.min(nearest) < NEAR, 1, 0))
    return found


def fill(points, base, columns, chunks, target, target_base, quad, height):
    for group in range(height // 8):
        block = points[pl.ds(base + group * 8, 8), :]
        rows = [
            [
                jnp.broadcast_to(block[:, axis * quad + a : axis * quad + a + 1], (8, 128))
                for axis in range(4)
            ]
            for a in range(quad)
        ]
        for place, chunk in enumerate(chunks):
            cols = [[columns[axis * quad + b, chunk] for axis in range(4)] for b in range(quad)]
            target[pl.ds(target_base + group * 8, 8), pl.ds(place * 128, 128)] = entries(rows, cols)


def order_kernel(
    sizes, pivots, column_geometry, columns, right, picks_root, picks_before, places, marks, landed, column_points
):
    row_count, col_count, tile, comps, slots = sizes
    quad = column_geometry.shape[1]
    lane_chunks = tile // 128
    for axis in range(4):
        column_points[pl.ds(axis * quad, quad), :] = column_geometry[axis]
    for a in range(quad):
        for b in range(quad):
            right[:, pl.ds((a * quad + b) * 2 * tile, 2 * tile)] = right_features(
                column_points[...], a, b
            )
    for axis in range(4):
        for b in range(quad):
            for chunk in range(2 * lane_chunks):
                part = column_geometry[axis, pl.ds(b, 1), pl.ds(chunk * 128, 128)]
                if axis < 3:
                    part = part * TURNS
                columns[axis * quad + b, chunk] = jnp.broadcast_to(part, (8, 128))
    piv = pivots[...]
    piv_col = as_column(piv)
    down = lax.broadcasted_iota(jnp.int32, (tile, tile), 0)
    across = lax.broadcasted_iota(jnp.int32, (tile, tile), 1)
    same = piv_col == piv
    earlier = down < across
    line = lax.broadcasted_iota(jnp.int32, (1, tile), 1)
    before = jnp.max(jnp.where(same & earlier, down, -1), axis=0, keepdims=True)
    after = jnp.max(jnp.where(same & (down > across), 1, 0), axis=0, keepdims=True)
    parent = jnp.max(jnp.where((piv_col == across) & earlier, down, -1), axis=0, keepdims=True)
    moved = jnp.max(parent)
    root = jnp.where(parent >= 0, parent, line)

    def doubled(carry):
        _, now = carry
        new = select_dot(jnp.broadcast_to(now, (8, tile)).astype(jnp.float32), chosen_where(down == now))
        new = new[:1].astype(jnp.int32)
        return jnp.max(jnp.where(new != now, 1, 0)), new

    _, root = lax.while_loop(lambda carry: carry[0] > 0, doubled, (jnp.where(moved >= 0, 1, 0), root))
    picks_root[...] = chosen_where(down == root)
    picks_before[...] = chosen_where(down == before)
    owner_row, owner_col, local, lanes = pivot_place(piv, tile, row_count, col_count)
    mine = (owner_row == lax.axis_index("row")) & (owner_col == lax.axis_index("col"))
    mine = mine & (after == 0) & (piv >= tile)
    place = chosen_where(as_column(lanes) == across)
    places[...] = place
    count = landed.shape[0]
    rows = [jnp.broadcast_to(jnp.where(mine & (local == k), 1.0, 0.0), (comps, tile)) for k in range(count)]
    rows.append(jnp.broadcast_to(jnp.where(before >= 0, 1.0, 0.0), (comps, tile)))
    for k, row in enumerate(rows):
        marks[k] = row
    hits = jnp.dot(
        jnp.concatenate(rows[:count], axis=0).astype(jnp.bfloat16), place, preferred_element_type=jnp.float32
    )
    for k in range(count):
        landed[k] = hits[k * comps : (k + 1) * comps]


def early_kernel(sizes, arrived, table, lower_inv, upper_inv, owned, lower, upper):
    row_count, col_count, tile, comps, slots = sizes
    me_row = lax.axis_index("row")
    for source in range(row_count):
        for s in range(slots):
            number = table[source, s, me_row]

            @pl.when(number & 1 == 0)
            def _():
                owned[lax.shift_right_logical(number, 1)] = arrived[source, pl.ds(s * comps, comps), :]

    lower[0], lower[1] = two_parts(lower_inv[...])
    upper[0], upper[1] = two_parts(upper_inv[...])


def main_kernel(
    sizes, owned, shared, passed, columns, right, picks_root, picks_before, places, marks, landed, lower, upper,
    slab, upper_block, points, filled, right_high, right_low, left, *squares,
):
    row_count, col_count, tile, comps, slots = sizes
    quad = 2 * comps // 8
    me_row = lax.axis_index("row")
    me_col = lax.axis_index("col")
    t = pl.program_id(0)
    tile_rows = pl.num_programs(0)
    lane_chunks = tile // 128
    height = HEIGHT
    steps = tile // height
    everything = range(2 * lane_chunks)

    def distances(block, buffer, chunks=everything):
        rows = left[pl.ds(pl.multiple_of(block * height, height), height), :]
        width = len(chunks) * 128
        for pair in range(quad * quad):
            lanes = pl.ds(pair * 2 * tile + chunks[0] * 128, width)
            buffer[:, lanes] = jnp.dot(rows, right[:, lanes], preferred_element_type=jnp.float32)

    def sweep(tile_index, chunks, last):
        def again(index, part):
            base = pl.multiple_of(index * height + part * PART, PART)
            fill(points.at[tile_index], base, columns, chunks, filled, base, quad, PART)

        def checked(index, near):
            total = functools.reduce(jnp.add, near)

            @pl.when(total > 0)
            def _():
                for place, flag in enumerate(near):

                    @pl.when(flag > 0)
                    def _():
                        again(index + place // (height // PART), place % (height // PART))

        def step(pair, near):
            index = 2 * pair
            checked(index - 2, near)
            flat = tile_index * steps + index
            found = []
            for part, (ahead, here) in enumerate(((squares[1], squares[0]), (squares[0], squares[1]))):
                distances(jnp.minimum(flat + 1 + part, last), ahead, chunks)
                base = pl.multiple_of((index + part) * height, height)
                found.extend(
                    quick_fill(
                        here, points.at[tile_index], base, columns, chunks, filled, base, quad, height
                    )
                )
            return tuple(found)

        checked(steps - 2, lax.fori_loop(0, steps // 2, step, (0,) * (2 * height // PART)))

    @pl.when(t == 0)
    def _():
        top = shared[pl.ds(0, comps), :] + passed[pl.ds(0, comps), :]
        chosen = shared[pl.ds(comps, comps), :] + passed[pl.ds(comps, comps), :]
        count = owned.shape[0]
        carried = select_dot(top, picks_root[...])
        again = select_dot(carried, picks_before[...])
        new_top = jnp.where(marks[count] > 0.5, again, chosen)
        sent = select_dot(
            jnp.concatenate([marks[k] * carried for k in range(count)], axis=0), places[...]
        )
        factor = jnp.where(
            lax.broadcasted_iota(jnp.int32, (comps, tile), 0) < 3 * quad, TURNS, WEIGHT
        )
        leading = jnp.full((comps, tile), (me_row == 0) & (me_col == 0))
        for k in range(count):
            fresh = sent[k * comps : (k + 1) * comps]
            hit = landed[k] > 0.5
            mixed = jnp.where(hit, fresh, owned[k])
            if k == 0:
                mixed = jnp.where(leading, new_top, mixed)
            points[k] = jnp.transpose(mixed * factor)
            left[pl.ds(k * tile, tile), :] = left_features(mixed)
        points[count] = jnp.transpose(new_top * factor)
        left[pl.ds(count * tile, tile), :] = left_features(new_top)
        distances(count * steps, squares[0], everything[lane_chunks:])
        sweep(count, everything[lane_chunks:], count * steps + steps - 1)
        distances(0, squares[0])
        solved = split_dot((lower[0], lower[1]), two_parts(filled[:, :tile]))
        upper_block[...] = solved
        high, low = two_parts(-split_dot((upper[0], upper[1]), two_parts(solved)))
        right_high[:, :tile], right_high[:, tile:] = upper[0], high
        right_low[:, :tile], right_low[:, tile:] = upper[1], low

    sweep(t, everything, tile_rows * steps - 1)
    high, low = two_parts(filled[:, :tile])
    dot = functools.partial(jnp.dot, preferred_element_type=jnp.float32)
    product = dot(high, right_low[...]) + dot(low, right_high[...]) + dot(high, right_high[...])
    slab[:, :tile] = product[:, :tile]
    slab[:, tile:] = product[:, tile:] + filled[:, tile:]


def per_device(row_geometry, column_geometry, octree_slot, pivots, lower_inv, upper_inv):
    row_count = lax.axis_size("row")
    col_count = lax.axis_size("col")
    tile = pivots.shape[0]
    slots_all, axes, quad = row_geometry.shape[2:5]
    slots = slots_all // row_count
    tile_rows = slots_all // 2
    comps = axes * quad
    sizes = (row_count, col_count, tile, comps, slots)
    geometry = row_geometry[0, 0]
    table = jnp.swapaxes(octree_slot[0], 1, 2)
    pivot_row = pivots.reshape(1, tile)
    vmem = pl.BlockSpec(memory_space=pltpu.VMEM)
    smem = pl.BlockSpec(memory_space=pltpu.SMEM)
    depth = (slots + 2) * comps
    packed = pl.pallas_call(
        functools.partial(pack_kernel, sizes),
        out_shape=pltpu.VMEM((row_count, depth, tile), jnp.float32),
        in_specs=[vmem, smem, vmem],
        out_specs=vmem,
        scratch_shapes=[pltpu.VMEM((slots_all * comps, tile), jnp.float32)],
        name="pack",
    )(geometry, table, pivot_row)
    arrived = lax.all_to_all(packed, "row", 0, 0, tiled=True)
    shared = jnp.sum(arrived[:, slots * comps :, :], axis=0)
    keep = functools.partial(pltpu.with_memory_space_constraint, memory_space=pltpu.VMEM)
    ready = pl.pallas_call(
        functools.partial(early_kernel, sizes),
        out_shape=(
            pltpu.VMEM((tile_rows, comps, tile), jnp.float32),
            pltpu.VMEM((2, tile, tile), jnp.bfloat16),
            pltpu.VMEM((2, tile, tile), jnp.bfloat16),
        ),
        in_specs=[vmem, smem, vmem, vmem],
        out_specs=(vmem,) * 3,
        name="early",
    )(keep(arrived), table, lower_inv, upper_inv)
    passed = jnp.zeros_like(shared)
    step = 1
    while step < col_count:
        partner = [(j, j ^ step) for j in range(col_count)]
        passed = lax.ppermute(shared, "col", partner)
        step *= 2
        if step < col_count:
            shared = shared + passed
            shared, ready = lax.optimization_barrier((shared, ready))
    order = pl.pallas_call(
        functools.partial(order_kernel, sizes),
        out_shape=(
            pltpu.VMEM((comps, 2 * tile // 128, 8, 128), jnp.float32),
            pltpu.VMEM((12 * comps, quad * quad * 2 * tile), jnp.bfloat16),
            pltpu.VMEM((tile, tile), jnp.bfloat16),
            pltpu.VMEM((tile, tile), jnp.bfloat16),
            pltpu.VMEM((tile, tile), jnp.bfloat16),
            pltpu.VMEM((tile_rows + 1, comps, tile), jnp.float32),
            pltpu.VMEM((tile_rows, comps, tile), jnp.float32),
        ),
        in_specs=[vmem, vmem],
        out_specs=(vmem,) * 7,
        scratch_shapes=[pltpu.VMEM((comps, 2 * tile), jnp.float32)],
        name="order",
    )(pivot_row, column_geometry)
    owned, lower, upper = map(keep, ready)
    slab, upper_block = pl.pallas_call(
        functools.partial(main_kernel, sizes),
        grid=(tile_rows,),
        out_shape=(
            jax.ShapeDtypeStruct((tile_rows * tile, 2 * tile), jnp.float32),
            jax.ShapeDtypeStruct((tile, tile), jnp.float32),
        ),
        in_specs=[vmem] * 12,
        out_specs=(
            pl.BlockSpec((tile, 2 * tile), lambda t: (t, 0)),
            pl.BlockSpec((tile, tile), lambda t: (0, 0)),
        ),
        scratch_shapes=[
            pltpu.VMEM((tile_rows + 1, tile, comps), jnp.float32),
            pltpu.VMEM((tile, 2 * tile), jnp.float32),
            pltpu.VMEM((tile, 2 * tile), jnp.bfloat16),
            pltpu.VMEM((tile, 2 * tile), jnp.bfloat16),
            pltpu.VMEM(((tile_rows + 1) * tile, 12 * comps), jnp.bfloat16),
            pltpu.VMEM((HEIGHT, quad * quad * 2 * tile), jnp.float32),
            pltpu.VMEM((HEIGHT, quad * quad * 2 * tile), jnp.float32),
        ],
        name="panel",
        compiler_params=pltpu.CompilerParams(),
    )(owned, keep(shared), keep(passed), *map(keep, order), lower, upper)
    return (slab.reshape(1, 1, tile_rows, tile, 2 * tile), upper_block)


def solution(mesh):
    placed = (
        P("col", "row", None, None, None, None),
        P(),
        P("col", None, None, None),
        P(),
        P(),
        P(),
    )
    return jax.shard_map(
        per_device,
        mesh=mesh,
        in_specs=placed,
        out_specs=(P("row", "col", None, None, None), P()),
        check_vma=False,
    )
```
